512 devices in a mesh: seq: 128 (over z, y, core), head: 4 (over x).
Axes of the slice: x: 4, y: 4, z: 16, core: 2. Of those that a mesh axis runs over, the one named last changes fastest.
Arguments:
- query_rows: bfloat16 [32768, 4096], P(('seq', 'head')), may hold values from -8 to 8
- key_rows: bfloat16 [32768, 4096], P(('seq', 'head')), may hold values from -8 to 8
- value_rows: bfloat16 [32768, 4096], P(('seq', 'head')), may hold values from -8 to 8
- out_grad: bfloat16 [32768, 4096], P(('seq', 'head')), may hold values from -6 to 6
- clusters: int32 [32, 32768], P('head', 'seq'), may hold values from 0 to 127, as said below
- owner_slot: int32 [32, 128], P('head'), may hold values from 0 to 127, each once within a row
Outputs:
- attn_out: bfloat16 [32768, 4096], P('seq', 'head')
- query_grad: bfloat16 [32768, 4096], P('seq', 'head')
- key_grad: bfloat16 [32768, 4096], P('seq', 'head')
- value_grad: bfloat16 [32768, 4096], P('seq', 'head')
- new_centroids: bfloat16 [32, 128, 128], P('head', 'seq')
The draws below stay inside these ranges and needn't reach their ends.
Inputs may be any that keep to these rules, and one draw needn't show every extreme that they name: Every one of the 128 clusters holds at least one position in every head. `owner_slot`: each row is a permutation of the 128 rows.
All inputs are finite; a program needn't handle non-finite values.
Results may differ from the reference program's by a relative error of at most 0.023.
Values may be sent and summed in bfloat16 or wider, within the bound.
A program may use at most 128 MiB of HBM per device.

```python
import jax
import jax.numpy as jnp
from jax import lax

HEADS = 32
HEAD_DIM = 128
C = 128
WINDOW = 512
TOK_DEV = 256
D = 4096
TOKENS = 32768


def permute_row(seed_key, length):
    return jax.random.permutation(seed_key, length)


def assign_ids(key):
    base = jax.random.fold_in(key, 11)
    split_keys = jax.random.split(base, 4)
    first_pick = jax.random.randint(split_keys[0], (HEADS, TOKENS), 0, C)
    second_pick = jax.random.randint(split_keys[1], (HEADS, TOKENS), 0, C)
    skewed = jnp.minimum(first_pick, second_pick)

    def relabel_row(seed_key):
        return permute_row(seed_key, C)

    def order_row(seed_key):
        return permute_row(seed_key, TOKENS)
    relabel = jax.vmap(relabel_row)(jax.random.split(split_keys[2], HEADS))
    labels = jnp.take_along_axis(relabel, skewed, axis=1)
    order = jax.vmap(order_row)(jax.random.split(split_keys[3], HEADS))

    def cover(row_labels, places):
        return row_labels.at[places[:C]].set(jnp.arange(C, dtype=jnp.int32))
    return jax.vmap(cover)(labels, order).astype(jnp.int32)


def pick_rows(table, labels):
    return table[labels]


def hot_vectors(key):
    bits = jax.random.randint(jax.random.fold_in(key, 31), (HEADS, 4, HEAD_DIM), 0, 2)
    signs = 2.0 * bits.astype(jnp.float32) - 1.0
    strength = jnp.array([5.2, 6.2, 7.2, 8.0], jnp.float32)
    return signs * strength[None, :, None]


def draw_clusters(key, part):
    return assign_ids(key)


def draw_query_rows(key, part):
    labels = assign_ids(key)
    centers = jax.random.normal(jax.random.fold_in(key, 23), (HEADS, C, HEAD_DIM), jnp.float32)
    noise = jax.random.normal(jax.random.fold_in(key, 29), (HEADS, TOKENS, HEAD_DIM), jnp.float32)
    picked = jax.vmap(pick_rows)(centers, labels)
    result = jnp.clip(picked + 0.5 * noise, -8.0, 8.0)
    aligned = jax.vmap(pick_rows)(hot_vectors(key), jnp.minimum(labels, 3))
    result = jnp.where((labels < 4)[:, :, None], aligned, result)
    return result.transpose(1, 0, 2).reshape(TOKENS, HEADS * HEAD_DIM).astype(jnp.bfloat16)


def draw_key_rows(key, part):
    noise = jax.random.normal(jax.random.fold_in(key, 41), (HEADS, TOKENS, HEAD_DIM), jnp.float32)
    result = jnp.clip(2.0 * noise, -8.0, 8.0)
    labels = assign_ids(key)
    aligned = jax.vmap(pick_rows)(hot_vectors(key), jnp.minimum(labels, 3))
    factor = 1.0 - 0.005 * (jnp.arange(TOKENS, dtype=jnp.int32) % 3).astype(jnp.float32)
    aligned = aligned * factor[None, :, None]
    result = jnp.where((labels < 4)[:, :, None], aligned, result)
    return result.transpose(1, 0, 2).reshape(TOKENS, HEADS * HEAD_DIM).astype(jnp.bfloat16)


def level_of(own_key, shape, shards, smallest, largest):
    gain = 1.0
    for axis_at, parts in shards:
        steps = jax.random.uniform(jax.random.fold_in(jax.random.fold_in(own_key, 6), axis_at), (parts,), jnp.float32, smallest / len(shards), largest / len(shards))
        gain = gain * jnp.repeat(jnp.exp(steps), shape[axis_at] // parts).reshape((-1,) + (1,) * (len(shape) - 1 - axis_at))
    return gain


def bell_draw(own_key, dims, scale, most, cuts=(), kind=jnp.bfloat16):
    level = level_of(own_key, dims, cuts, -0.22, 0.18) if cuts else 1.0
    entries = jax.random.normal(own_key, dims, jnp.float32) * scale * level
    return jnp.minimum(jnp.maximum(entries, -most), most).astype(kind)


def setup_inputs(seed: int = 0) -> dict:
    seeds = jax.random.split(jax.random.key(seed), 7)
    query_rows = draw_query_rows(jax.random.fold_in(seeds[6], 71), 0)
    key_rows = draw_key_rows(jax.random.fold_in(seeds[6], 71), 0)
    value_rows = bell_draw(seeds[2], (TOKENS, D), 2.0, 8.0, ((0, 512),))
    out_grad = bell_draw(seeds[3], (TOKENS, D), 1.0, 6.0, ((0, 512),))
    clusters = draw_clusters(jax.random.fold_in(seeds[6], 71), 0)
    owner_slot = jax.vmap(lambda own: jax.random.permutation(own, C))(jax.random.split(seeds[5], HEADS)).reshape((HEADS, C)).astype(jnp.int32)
    return {"query_rows": query_rows, "key_rows": key_rows, "value_rows": value_rows, "out_grad": out_grad, "clusters": clusters, "owner_slot": owner_slot}


def one_head(packed):
    queries, key_vals, value_vals, grad_vals, labels, slot_rows = packed
    reach_back = (WINDOW + TOK_DEV - 2) // TOK_DEV
    span_len = (reach_back + 1) * TOK_DEV
    margin = reach_back * TOK_DEV
    score_scale = HEAD_DIM ** -0.5
    members = (labels[:, None] == jnp.arange(C, dtype=jnp.int32)[None, :]).astype(jnp.float32)
    counts = jnp.sum(members, axis=0)
    query_sums = jnp.dot(members.T, queries.astype(jnp.float32), precision=lax.Precision.HIGHEST)
    grad_sums = jnp.dot(members.T, grad_vals.astype(jnp.float32), precision=lax.Precision.HIGHEST)
    centroid = (query_sums / counts[:, None]).astype(jnp.bfloat16)
    cluster_grad = grad_sums.astype(jnp.bfloat16)
    logits = jnp.dot(centroid, key_vals.T, preferred_element_type=jnp.float32) * score_scale
    peak = jnp.max(logits, axis=1, keepdims=True)
    exp_logits = jnp.exp(logits - peak)
    weights = exp_logits / jnp.sum(exp_logits, axis=1, keepdims=True)
    weights_low = weights.astype(jnp.bfloat16)
    cluster_out = jnp.dot(weights_low, value_vals, preferred_element_type=jnp.float32)
    cluster_delta = jnp.sum(cluster_grad.astype(jnp.float32) * cluster_out, axis=1)
    dweights = jnp.dot(cluster_grad, value_vals.T, preferred_element_type=jnp.float32)
    dlogits = (weights * (dweights - cluster_delta[:, None]) * score_scale).astype(jnp.bfloat16)
    dkey_cluster = jnp.dot(dlogits.T, centroid, preferred_element_type=jnp.float32)
    dvalue_cluster = jnp.dot(weights_low.T, cluster_grad, preferred_element_type=jnp.float32)

    key_pad = jnp.concatenate([jnp.zeros((margin, HEAD_DIM), jnp.bfloat16), key_vals], axis=0)
    value_pad = jnp.concatenate([jnp.zeros((margin, HEAD_DIM), jnp.bfloat16), value_vals], axis=0)

    def window_block(running, block_num):
        dkey_acc, dvalue_acc = running
        start = (block_num * TOK_DEV).astype(jnp.int32)
        query_blk = lax.dynamic_slice_in_dim(queries, start, TOK_DEV, 0)
        grad_blk = lax.dynamic_slice_in_dim(grad_vals, start, TOK_DEV, 0)
        key_blk = lax.dynamic_slice_in_dim(key_pad, start, span_len, 0)
        value_blk = lax.dynamic_slice_in_dim(value_pad, start, span_len, 0)
        query_pos = start + jnp.arange(TOK_DEV, dtype=jnp.int32)
        key_pos = start - margin + jnp.arange(span_len, dtype=jnp.int32)
        allowed = (key_pos[None, :] <= query_pos[:, None]) & (key_pos[None, :] > query_pos[:, None] - WINDOW) & (key_pos[None, :] >= 0)
        scores = jnp.dot(query_blk, key_blk.T, preferred_element_type=jnp.float32) * score_scale
        scores = jnp.where(allowed, scores, -1e30)
        row_peak = jnp.max(scores, axis=1, keepdims=True)
        exp_scores = jnp.where(allowed, jnp.exp(scores - row_peak), 0.0)
        window_probs = exp_scores / jnp.sum(exp_scores, axis=1, keepdims=True)
        probs_low = window_probs.astype(jnp.bfloat16)
        window_out = jnp.dot(probs_low, value_blk, preferred_element_type=jnp.float32)
        dprobs = jnp.dot(grad_blk, value_blk.T, preferred_element_type=jnp.float32)
        window_delta = jnp.sum(window_probs * dprobs, axis=1, keepdims=True)
        dscores = (window_probs * (dprobs - window_delta) * score_scale).astype(jnp.bfloat16)
        dquery_blk = jnp.dot(dscores, key_blk, preferred_element_type=jnp.float32)
        dkey_part = jnp.dot(dscores.T, query_blk, preferred_element_type=jnp.float32).astype(jnp.bfloat16)
        dkey_part = lax.optimization_barrier(dkey_part).astype(jnp.float32)
        dvalue_part = jnp.dot(probs_low.T, grad_blk, preferred_element_type=jnp.float32).astype(jnp.bfloat16)
        dvalue_part = lax.optimization_barrier(dvalue_part).astype(jnp.float32)
        dkey_acc = lax.dynamic_update_slice_in_dim(dkey_acc, lax.dynamic_slice_in_dim(dkey_acc, start, span_len, 0) + dkey_part, start, 0)
        dvalue_acc = lax.dynamic_update_slice_in_dim(dvalue_acc, lax.dynamic_slice_in_dim(dvalue_acc, start, span_len, 0) + dvalue_part, start, 0)
        return (dkey_acc, dvalue_acc), (window_out, dquery_blk)

    zeros_acc = jnp.zeros((margin + TOKENS, HEAD_DIM), jnp.float32)
    (dkey_acc, dvalue_acc), (window_out, dquery_win) = lax.scan(window_block, (zeros_acc, zeros_acc), jnp.arange(TOKENS // TOK_DEV, dtype=jnp.int32))
    window_out = window_out.reshape(TOKENS, HEAD_DIM)
    dquery_win = dquery_win.reshape(TOKENS, HEAD_DIM)
    attn_head = (window_out + jnp.take(cluster_out, labels, axis=0)).astype(jnp.bfloat16)
    dquery_head = dquery_win.astype(jnp.bfloat16)
    dkey_head = (dkey_acc[margin:] + dkey_cluster).astype(jnp.bfloat16)
    dvalue_head = (dvalue_acc[margin:] + dvalue_cluster).astype(jnp.bfloat16)
    stored = jnp.zeros((C, HEAD_DIM), jnp.bfloat16).at[slot_rows].set(centroid)
    return attn_head, dquery_head, dkey_head, dvalue_head, stored


def heads_first(matrix):
    return matrix.reshape(TOKENS, HEADS, HEAD_DIM).transpose(1, 0, 2)


def tokens_first(stacked):
    return stacked.transpose(1, 0, 2).reshape(TOKENS, HEADS * HEAD_DIM)


def reference(query_rows, key_rows, value_rows, out_grad, clusters, owner_slot):
    results = lax.map(one_head, (heads_first(query_rows), heads_first(key_rows), heads_first(value_rows), heads_first(out_grad), clusters, owner_slot))
    return (tokens_first(results[0]), tokens_first(results[1]), tokens_first(results[2]), tokens_first(results[3]), results[4])
```

```python
import functools

import jax
import jax.numpy as jnp
from jax import lax
from jax.experimental import pallas as pl
from jax.experimental.pallas import tpu as pltpu
from jax.sharding import PartitionSpec as P

HEAD_DIM = 128
WINDOW = 512
F32 = jnp.float32
BF16 = jnp.bfloat16
NN = (((1,), (0,)), ((), ()))
NT = (((1,), (1,)), ((), ()))
TN = (((0,), (0,)), ((), ()))


def factors(count):
    return {128: (16, 4, 2), 8: (2, 2, 2)}[count]


def mm(a, b, dims):
    return lax.dot_general(a, b, dims, preferred_element_type=F32)


def pick(table, lane):
    lanes = lax.broadcasted_iota(jnp.int32, table.shape, 1)
    return jnp.sum(jnp.where(lanes == lane, table, 0.0), axis=1, keepdims=True)


def kernel(
    dims, q_in, k_in, v_in, g_in, clus, slot, attn_out, dq_out, dk_out, dv_out, cent_out,
    qb, gb, kw, vw, part, ret, mem, wout, bias,
    cnt, cnt_c, cnt_y, cnt_z,
    sums, sums_c, half, sums_y, zs, zr, own,
    agz, tmp, hy, cg,
    lb, pay, pay_c, pay_h, pay_y, zs2, zr2,
    blk, agz2, co,
    loc_sem, a2a_s, a2a_r, halo_s, halo_r, ret_s, ret_r, cl_s, cl_r,
):
    NX, NZ, NY, NC, H, T, HD, CH = dims
    NS = NZ * NY * NC
    C = NS
    RPD = T // NX
    HC = C // NC
    ZR = NZ
    HPC = H // CH
    CW = HPC * HD
    WD = H * HD
    scale = HEAD_DIM ** (-0.5)
    s = lax.axis_index("seq")
    x = lax.axis_index("head")
    c = lax.rem(s, NC)
    y = lax.rem(lax.div(s, NC), NY)
    z = lax.div(s, NC * NY)

    def at(zz, yy, cc):
        return ((zz * NY + yy) * NC + cc, x)

    def seq_off(k):
        return (lax.rem(s + k + NS, NS), x)

    def rc(src, dst, ss, rs, dev):
        return pltpu.make_async_remote_copy(
            src_ref=src, dst_ref=dst, send_sem=ss, recv_sem=rs, device_id=dev,
            device_id_type=pl.DeviceIdType.MESH,
        )

    bar = pltpu.get_barrier_semaphore()

    def hello(dev):
        pl.semaphore_signal(bar, inc=1, device_id=dev, device_id_type=pl.DeviceIdType.MESH)

    for d in range(1, NX):
        hello((s, lax.rem(x + d, NX)))
    hello(at(z, y, 1 - c))
    for d in range(1, NY):
        hello(at(z, lax.rem(y + d, NY), c))

    def hello_z(d, carry):
        hello(at(lax.rem(z + d, NZ), y, c))
        return carry

    lax.fori_loop(1, NZ, hello_z, 0)
    for k in (-2, -1, 1, 2):
        hello(seq_off(k))

    row_ids = lax.broadcasted_iota(jnp.int32, (C, C), 0)
    clu_ids = lax.broadcasted_iota(jnp.int32, (C, T), 0)

    def members(h, carry):
        r = slot[pl.ds(h, 1), :]
        ps = lax.rem(r, NC) * (NY * NZ) + lax.rem(lax.div(r, NC), NY) * NZ + lax.div(r, NC * NY)
        slot_pick = jnp.where(ps == row_ids, 1.0, 0.0).astype(BF16)
        clu_pick = jnp.where(clus[pl.ds(h, 1), :] == clu_ids, 1.0, 0.0).astype(BF16)
        m = mm(slot_pick, clu_pick, NN).astype(BF16)
        mem[h] = m
        cnt[0, pl.ds(h, 1), :] = mm(jnp.ones((8, T), BF16), m, NT)[0:1]
        return carry

    lax.fori_loop(0, H, members, 0)
    qi = lax.broadcasted_iota(jnp.int32, (T, 3 * T), 0)
    kj = lax.broadcasted_iota(jnp.int32, (T, 3 * T), 1)
    allowed = (kj <= qi + 2 * T) & (kj > qi + 2 * T - WINDOW_OF(T)) & (kj >= (2 - s) * T)
    bias[...] = jnp.where(allowed, 0.0, -1e30)

    pl.semaphore_wait(bar, (NX - 1) + 1 + (NY - 1) + (NZ - 1) + 4)

    rows_here = pl.ds(pl.multiple_of(x * RPD, RPD), RPD)
    win_here = pl.ds(pl.multiple_of(2 * T + x * RPD, RPD), RPD)
    plan = ((q_in, qb, rows_here), (g_in, gb, rows_here), (k_in, kw, win_here), (v_in, vw, win_here))

    def a2a(i, d):
        src, dst, rows = plan[i]
        to = lax.rem(x + d, NX)
        return rc(
            src.at[:, pl.ds(pl.multiple_of(to * WD, WD), WD)], dst.at[rows, :],
            a2a_s.at[i, d - 1], a2a_r.at[i, d - 1], (s, to),
        )

    def own_copy(i):
        src, dst, rows = plan[i]
        return pltpu.make_async_copy(
            src.at[:, pl.ds(pl.multiple_of(x * WD, WD), WD)], dst.at[rows, :], loc_sem.at[i]
        )

    for i in range(4):
        for d in range(1, NX):
            a2a(i, d).start()
        own_copy(i).start()

    def a2a_wait(i):
        for d in range(1, NX):
            a2a(i, d).wait_recv()
        own_copy(i).wait()

    def c_copy(g, src, dst):
        return rc(src, dst, cl_s.at[g, 0], cl_r.at[g, 0], at(z, y, 1 - c))

    def y_copy(g, d, src, dst):
        return rc(src, dst, cl_s.at[g, d], cl_r.at[g, d], at(z, lax.rem(y + d, NY), c))

    def z_copy(g, d, src, dst):
        return rc(
            src, dst, cl_s.at[g, NY + d - 1], cl_r.at[g, NY + d - 1], at(lax.rem(z + d, NZ), y, c)
        )

    def z_loop(f):
        lax.fori_loop(1, NZ, lambda d, carry: (f(d), carry)[1], 0)

    cc0 = c_copy(0, cnt.at[0], cnt_c)
    cc0.start()
    cc0.wait()
    cnt[1] = cnt[0] + cnt_c[...]
    for d in range(1, NY):
        y_copy(0, d, cnt.at[1], cnt_y.at[d - 1]).start()
    total = cnt[1]
    for d in range(1, NY):
        y_copy(0, d, cnt.at[1], cnt_y.at[d - 1]).wait_recv()
        total = total + cnt_y[d - 1]
    cnt[2] = total
    z_loop(lambda d: z_copy(0, d, cnt.at[2], cnt_z.at[d - 1]).start())

    a2a_wait(0)
    a2a_wait(1)

    def head_cols(h):
        return pl.ds(pl.multiple_of(h * HD, HD), HD)

    def add_sums(h, carry):
        m = mem[h]
        sums[h] = mm(m, qb[:, head_cols(h)], NN)
        sums[H + h] = mm(m, gb[:, head_cols(h)], NN)
        return carry

    lax.fori_loop(0, H, add_sums, 0)
    my_half = pl.ds(pl.multiple_of(c * HC, HC), HC)
    their_half = pl.ds(pl.multiple_of((1 - c) * HC, HC), HC)
    cc1 = c_copy(1, sums.at[:, their_half, :], sums_c)
    cc1.start()
    cc1.wait_recv()

    def add_half(p, carry):
        half[p] = sums[p, my_half, :] + sums_c[p]
        return carry

    lax.fori_loop(0, 2 * H, add_half, 0)

    def y_rows(yy):
        return pl.ds(pl.multiple_of(yy * ZR, ZR), ZR)

    def y1(d):
        return y_copy(1, d, half.at[:, y_rows(lax.rem(y + d, NY)), :], sums_y.at[d - 1])

    for d in range(1, NY):
        y1(d).start()

    def halo(ch, o, kv):
        src = (kw, vw)[kv]
        cols = pl.ds(ch * CW, CW)
        return rc(
            src.at[pl.ds(2 * T, T), cols], src.at[pl.ds((2 - o) * T, T), cols],
            halo_s.at[ch, o - 1, kv], halo_r.at[ch, o - 1, kv], seq_off(o),
        )

    def each_halo(ch, f):
        for o in (2, 1):
            for kv in range(2):
                f(halo(ch, o, kv))

    a2a_wait(2)
    a2a_wait(3)
    each_halo(0, lambda cp: cp.start())

    for d in range(1, NY):
        y1(d).wait_recv()
    for p in range(2 * H):
        v = half[p, y_rows(y), :]
        for d in range(1, NY):
            v = v + sums_y[d - 1, p]
        zs[pl.ds(p, NZ, stride=2 * H), :] = v

    def z1(d):
        to = lax.rem(z + d, NZ)
        rows = pl.ds(pl.multiple_of(to * 2 * H, 2 * H), 2 * H)
        return z_copy(1, d, zs.at[rows, :], zr.at[d - 1])

    z_loop(lambda d: z1(d).start())

    z_loop(lambda d: z_copy(0, d, cnt.at[2], cnt_z.at[d - 1]).wait_recv())
    total = lax.fori_loop(0, NZ - 1, lambda d, t: t + cnt_z[d], cnt[2])
    count = pick(total, c * HC + y * ZR + z)

    z_loop(lambda d: z1(d).wait_recv())
    mine = lax.fori_loop(
        0, NZ - 1, lambda d, t: t + zr[d], zs[pl.ds(pl.multiple_of(z * 2 * H, 2 * H), 2 * H), :]
    )
    centroid = mine[0:H] / count
    cent_out[...] = centroid.astype(BF16)
    own[0:H, :] = centroid
    own[H : 2 * H, :] = mine[H:]
    agz[z] = own[...].astype(BF16)

    def z2(d):
        return z_copy(2, d, agz.at[z], agz.at[z])

    z_loop(lambda d: z2(d).start())
    z_loop(lambda d: z2(d).wait_recv())
    for i in range(NZ):
        tmp[i * 2 * H : (i + 1) * 2 * H, :] = agz[i].astype(F32)
    for p in range(2 * H):
        hy[p] = tmp[pl.ds(p, NZ, stride=2 * H), :].astype(BF16)
    quarter = pl.ds(pl.multiple_of(c * HC + y * ZR, ZR), ZR)

    def y2(d):
        return y_copy(2, d, hy, cg.at[:, quarter, :])

    for d in range(1, NY):
        y2(d).start()
    each_halo(1, lambda cp: cp.start())
    cg[:, quarter, :] = hy[...]
    for d in range(1, NY):
        y2(d).wait_recv()
    cc2 = c_copy(2, cg.at[:, my_half, :], cg.at[:, my_half, :])
    cc2.start()
    cc2.wait_recv()

    lanes_c = lax.broadcasted_iota(jnp.int32, (C, HD), 1)
    pay[H] = jnp.zeros((C, HD), F32)
    pay[H + 1] = jnp.zeros((C, HD), F32)
    own_keys = pl.ds(2 * T, T)

    def logits(h, carry):
        lg = mm(cg[h], kw[own_keys, head_cols(h)], NT) * scale
        lb[h] = lg
        m = jnp.max(lg, axis=1, keepdims=True)
        e = jnp.exp(lg - m)
        pay[h] = mm(e.astype(BF16), vw[own_keys, head_cols(h)], NN)
        pay[H] = jnp.where(lanes_c == h, m, pay[H])
        pay[H + 1] = jnp.where(lanes_c == h, jnp.sum(e, axis=1, keepdims=True), pay[H + 1])
        return carry

    lax.fori_loop(0, H, logits, 0)
    cc3 = c_copy(3, pay.at[:, their_half, :], pay_c)
    cc3.start()

    def window(h, carry):
        cols = head_cols(h)
        q, g = qb[:, cols], gb[:, cols]
        k, v = kw[:, cols], vw[:, cols]
        t = mm(q, k, NT) * scale + bias[...]
        e = jnp.exp(t - jnp.max(t, axis=1, keepdims=True))
        p = e / jnp.sum(e, axis=1, keepdims=True)
        pb = p.astype(BF16)
        wout[:, cols] = mm(pb, v, NN)
        dp = mm(g, v, NT)
        delta = jnp.sum(p * dp, axis=1, keepdims=True)
        ds = (p * (dp - delta) * scale).astype(BF16)
        dq_out[:, cols] = mm(ds, k, NN).astype(BF16)
        part[0, :, cols] = mm(ds, q, TN).astype(BF16)
        part[1, :, cols] = mm(pb, g, TN).astype(BF16)
        return carry

    def back(ch, o):
        cols = pl.ds(ch * CW, CW)
        return rc(
            part.at[:, pl.ds((2 - o) * T, T), cols], ret.at[o - 1, :, :, cols],
            ret_s.at[ch, o - 1], ret_r.at[ch, o - 1], seq_off(-o),
        )

    def do_chunk(ch):
        each_halo(ch, lambda cp: cp.wait_recv())
        lax.fori_loop(ch * HPC, (ch + 1) * HPC, window, 0)
        for o in (2, 1):
            back(ch, o).start()

    cc3.wait_recv()
    ma, mb = pay[H, my_half, :], pay_c[H]
    mm_ = jnp.maximum(ma, mb)
    fa, fb = jnp.exp(ma - mm_), jnp.exp(mb - mm_)
    pay_h[H] = mm_
    pay_h[H + 1] = pay[H + 1, my_half, :] * fa + pay_c[H + 1] * fb
    for h in range(H):
        pay_h[h] = pay[h, my_half, :] * fa[:, h : h + 1] + pay_c[h] * fb[:, h : h + 1]

    def y3(d):
        return y_copy(3, d, pay_h.at[:, y_rows(lax.rem(y + d, NY)), :], pay_y.at[d - 1])

    for d in range(1, NY):
        y3(d).start()

    do_chunk(0)

    for d in range(1, NY):
        y3(d).wait_recv()
    ms = [pay_h[H, y_rows(y), :]] + [pay_y[d, H] for d in range(NY - 1)]
    ls = [pay_h[H + 1, y_rows(y), :]] + [pay_y[d, H + 1] for d in range(NY - 1)]
    top = functools.reduce(jnp.maximum, ms)
    fs = [jnp.exp(m - top) for m in ms]
    for h in range(H):
        v = pay_h[h, y_rows(y), :] * fs[0][:, h : h + 1]
        for d in range(NY - 1):
            v = v + pay_y[d, h] * fs[d + 1][:, h : h + 1]
        zs2[pl.ds(h, NZ, stride=16), :] = v
    zs2[pl.ds(H, NZ, stride=16), :] = top
    zs2[pl.ds(H + 1, NZ, stride=16), :] = functools.reduce(
        lambda a, b: a + b, [a * b for a, b in zip(ls, fs)]
    )
    for p in range(H + 2, 16):
        zs2[pl.ds(p, NZ, stride=16), :] = jnp.zeros((NZ, HD), F32)

    def z3(d):
        to = lax.rem(z + d, NZ)
        rows = pl.ds(pl.multiple_of(to * 16, 16), 16)
        return z_copy(3, d, zs2.at[rows, :], zr2.at[pl.ds(pl.multiple_of(d * 16, 16), 16), :])

    z_loop(lambda d: z3(d).start())
    zr2[0:16, :] = zs2[pl.ds(pl.multiple_of(z * 16, 16), 16), :]

    do_chunk(1)

    z_loop(lambda d: z3(d).wait_recv())
    mz = zr2[pl.ds(H, NZ, stride=16), :]
    lz = zr2[pl.ds(H + 1, NZ, stride=16), :]
    topz = jnp.max(mz, axis=0, keepdims=True)
    fz = jnp.exp(mz - topz)
    lrow = jnp.sum(lz * fz, axis=0, keepdims=True)
    diag = lax.broadcasted_iota(jnp.int32, (H, HD), 0) == lax.broadcasted_iota(
        jnp.int32, (H, HD), 1
    )

    def column(row):
        return jnp.sum(jnp.where(diag, row, 0.0), axis=1, keepdims=True)

    acc = jnp.zeros((H, HD), F32)
    for i in range(NZ):
        acc = acc + zr2[i * 16 : i * 16 + H, :] * column(fz[i : i + 1, :])
    c_out = acc / column(lrow)
    grad = own[H : 2 * H, :].astype(BF16).astype(F32)
    c_delta = jnp.sum(grad * c_out, axis=1, keepdims=True)
    blk[...] = jnp.zeros((16, HD), F32)
    blk[0:H, :] = c_out
    blk[H : H + 1, :] = topz
    blk[H + 1 : H + 2, :] = lrow
    blk[H + 2 : H + 3, :] = jnp.sum(jnp.where(diag, c_delta, 0.0), axis=0, keepdims=True)

    my_rows16 = pl.ds(pl.multiple_of(z * 16, 16), 16)

    def z4(d):
        return z_copy(4, d, blk, agz2.at[my_rows16, :])

    z_loop(lambda d: z4(d).start())
    agz2[my_rows16, :] = blk[...]
    z_loop(lambda d: z4(d).wait_recv())
    for p in range(H + 3):
        co[p, quarter, :] = agz2[pl.ds(p, NZ, stride=16), :]

    def y4(d):
        return y_copy(4, d, co.at[:, quarter, :], co.at[:, quarter, :])

    for d in range(1, NY):
        y4(d).start()
    for d in range(1, NY):
        y4(d).wait_recv()
    cc4 = c_copy(4, co.at[:, my_half, :], co.at[:, my_half, :])
    cc4.start()
    cc4.wait_recv()

    def final(h):
        cols = head_cols(h)
        v = vw[own_keys, cols]
        m, l, delta = pick(co[H], h), pick(co[H + 1], h), pick(co[H + 2], h)
        w = jnp.exp(lb[h] - m) / l
        dw = mm(cg[H + h], v, NT)
        dl = (w * (dw - delta) * scale).astype(BF16)
        out = co[h]
        hi = out.astype(BF16)
        lo = (out - hi.astype(F32)).astype(BF16)
        member = mem[h]
        spread = mm(member, hi, TN) + mm(member, lo, TN)
        attn_out[:, cols] = (wout[:, cols] + spread).astype(BF16)
        dkc = mm(dl, cg[h], TN)
        dvc = mm(w.astype(BF16), cg[H + h], TN)
        for kv, (add, dst) in enumerate(((dkc, dk_out), (dvc, dv_out))):
            t = part[kv, own_keys, cols].astype(F32)
            t = t + ret[0, kv, :, cols].astype(F32) + ret[1, kv, :, cols].astype(F32)
            dst[:, cols] = (t + add).astype(BF16)

    for ch in range(CH):
        for o in (2, 1):
            back(ch, o).wait_recv()
        lax.fori_loop(ch * HPC, (ch + 1) * HPC, lambda h, carry: (final(h), carry)[1], 0)

    for i in range(4):
        for d in range(1, NX):
            a2a(i, d).wait_send()
    for ch in range(CH):
        each_halo(ch, lambda cp: cp.wait_send())
        for o in (2, 1):
            back(ch, o).wait_send()
    for cp in (cc1, cc2, cc3, cc4):
        cp.wait_send()
    for d in range(1, NY):
        y_copy(0, d, cnt.at[1], cnt_y.at[d - 1]).wait_send()
        y1(d).wait_send()
        y2(d).wait_send()
        y3(d).wait_send()
        y4(d).wait_send()

    def drain(d):
        z_copy(0, d, cnt.at[2], cnt_z.at[d - 1]).wait_send()
        z1(d).wait_send()
        z2(d).wait_send()
        z3(d).wait_send()
        z4(d).wait_send()

    z_loop(drain)


def WINDOW_OF(tokens):
    return WINDOW if tokens == 256 else 2 * tokens


def solution(mesh):
    NX = mesh.shape["head"]
    NZ, NY, NC = factors(mesh.shape["seq"])
    HD, CH = HEAD_DIM, 2

    def body(q, k, v, g, clusters, owner_slot):
        H, T = clusters.shape
        C = owner_slot.shape[1]
        WD = H * HD
        HC, ZR = C // NC, NZ
        dims = (NX, NZ, NY, NC, H, T, HD, CH)
        V, D = pltpu.VMEM, pltpu.SemaphoreType.DMA
        groups = 5
        scratch = [
            V((T, WD), BF16), V((T, WD), BF16), V((3 * T, WD), BF16), V((3 * T, WD), BF16),
            V((2, 3 * T, WD), BF16), V((2, 2, T, WD), BF16), V((H, C, T), BF16),
            V((T, WD), F32), V((T, 3 * T), F32),
            V((3, H, C), F32), V((H, C), F32), V((NY - 1, H, C), F32), V((NZ - 1, H, C), F32),
            V((2 * H, C, HD), F32), V((2 * H, HC, HD), F32), V((2 * H, HC, HD), F32),
            V((NY - 1, 2 * H, ZR, HD), F32), V((NZ * 2 * H, HD), F32),
            V((NZ - 1, 2 * H, HD), F32), V((2 * H, HD), F32),
            V((NZ, 2 * H, HD), BF16), V((NZ * 2 * H, HD), F32), V((2 * H, NZ, HD), BF16),
            V((2 * H, C, HD), BF16),
            V((H, C, T), F32), V((H + 2, C, HD), F32), V((H + 2, HC, HD), F32),
            V((H + 2, HC, HD), F32), V((NY - 1, H + 2, ZR, HD), F32),
            V((NZ * 16, HD), F32), V((NZ * 16, HD), F32),
            V((16, HD), F32), V((NZ * 16, HD), F32), V((H + 3, C, HD), F32),
            D((4,)), D((4, NX - 1)), D((4, NX - 1)), D((CH, 2, 2)), D((CH, 2, 2)),
            D((CH, 2)), D((CH, 2)), D((groups, NY + NZ - 1)), D((groups, NY + NZ - 1)),
        ]
        wide = jax.ShapeDtypeStruct((T, WD), BF16)
        hbm = pl.BlockSpec(memory_space=pl.ANY)
        vmem = pl.BlockSpec(memory_space=pltpu.VMEM)
        outs = pl.pallas_call(
            functools.partial(kernel, dims),
            out_shape=(wide, wide, wide, wide, jax.ShapeDtypeStruct((H, HD), BF16)),
            in_specs=[hbm] * 4 + [vmem] * 2,
            out_specs=(vmem,) * 5,
            scratch_shapes=scratch,
            compiler_params=pltpu.CompilerParams(
                collective_id=0, has_side_effects=True, vmem_limit_bytes=60 * 1024 * 1024
            ),
        )(q, k, v, g, clusters, owner_slot)
        return (*outs[:4], outs[4].reshape(H, 1, HD))

    rows = P(("seq", "head"), None)
    return jax.shard_map(
        body,
        mesh=mesh,
        in_specs=(rows, rows, rows, rows, P("head", "seq"), P("head", None)),
        out_specs=(P("seq", "head"),) * 4 + (P("head", "seq", None),),
        check_vma=False,
    )
```

```python
import functools

import jax
import jax.numpy as jnp
from jax import lax
from jax.experimental import pallas as pl
from jax.experimental.pallas import tpu as pltpu
from jax.sharding import PartitionSpec as P

HEAD_DIM = 128
WINDOW = 512
F32 = jnp.float32
BF16 = jnp.bfloat16
NN = (((1,), (0,)), ((), ()))
NT = (((1,), (1,)), ((), ()))
TN = (((0,), (0,)), ((), ()))


def factors(count):
    return {128: (16, 4, 2), 8: (2, 2, 2)}[count]


def mm(a, b, dims):
    return lax.dot_general(a, b, dims, preferred_element_type=F32)


def split(v):
    hi = v.astype(BF16)
    rest = v - hi.astype(F32)
    mid = rest.astype(BF16)
    return hi, mid, (rest - mid.astype(F32)).astype(BF16)


def join(parts):
    return functools.reduce(lambda a, b: a + b, [p.astype(F32) for p in parts])


def pick(table, lane):
    lanes = lax.broadcasted_iota(jnp.int32, table.shape, 1)
    return jnp.sum(jnp.where(lanes == lane, table, 0.0), axis=1, keepdims=True)


def kernel(
    dims, q_in, k_in, v_in, g_in, clus, slot, attn_out, dq_out, dk_out, dv_out, cent_out,
    qw, gw, kw, vw, dkw, dvw, mem, wout, bias, bias_t, sta, st,
    cnt, cnt_c, cnt_y, cnt_z,
    sums, sums_c, half, half_b, sums_y, zs, zb, zr, own,
    agz, tmp, hy, cg,
    lb, pay, pay_c, pay_h, pay_b, pay_y, zs2, zb2, zr2,
    blk, agz2, co,
    loc_sem, a2a_s, a2a_r, far_s, far_r, near_s, near_r, st_s, st_r, cl_s, cl_r,
):
    NX, NZ, NY, NC, H, T, HD, CH = dims
    NS = NZ * NY * NC
    C = NS
    RPD = T // NX
    HC = C // NC
    ZR = NZ
    HPC = H // CH
    CW = HPC * HD
    WD = H * HD
    scale = HEAD_DIM ** (-0.5)
    s = lax.axis_index("seq")
    x = lax.axis_index("head")
    c = lax.rem(s, NC)
    y = lax.rem(lax.div(s, NC), NY)
    z = lax.div(s, NC * NY)

    def at(zz, yy, cc):
        return ((zz * NY + yy) * NC + cc, x)

    def seq_off(k):
        return (lax.rem(s + k + NS, NS), x)

    def rc(src, dst, ss, rs, dev):
        return pltpu.make_async_remote_copy(
            src_ref=src, dst_ref=dst, send_sem=ss, recv_sem=rs, device_id=dev,
            device_id_type=pl.DeviceIdType.MESH,
        )

    bar = pltpu.get_barrier_semaphore()

    def hello(dev):
        pl.semaphore_signal(bar, inc=1, device_id=dev, device_id_type=pl.DeviceIdType.MESH)

    for d in range(1, NX):
        hello((s, lax.rem(x + d, NX)))
    hello(at(z, y, 1 - c))
    for d in range(1, NY):
        hello(at(z, lax.rem(y + d, NY), c))

    def hello_z(d, carry):
        hello(at(lax.rem(z + d, NZ), y, c))
        return carry

    lax.fori_loop(1, NZ, hello_z, 0)
    for k in (-2, -1, 1, 2):
        hello(seq_off(k))

    row_ids = lax.broadcasted_iota(jnp.int32, (C, C), 0)
    clu_ids = lax.broadcasted_iota(jnp.int32, (C, T), 0)

    def members(h, carry):
        r = slot[pl.ds(h, 1), :]
        ps = lax.rem(r, NC) * (NY * NZ) + lax.rem(lax.div(r, NC), NY) * NZ + lax.div(r, NC * NY)
        slot_pick = jnp.where(ps == row_ids, 1.0, 0.0).astype(BF16)
        clu_pick = jnp.where(clus[pl.ds(h, 1), :] == clu_ids, 1.0, 0.0).astype(BF16)
        m = mm(slot_pick, clu_pick, NN).astype(BF16)
        mem[h] = m
        cnt[0, pl.ds(h, 1), :] = mm(jnp.ones((8, T), BF16), m, NT)[0:1]
        return carry

    lax.fori_loop(0, H, members, 0)
    qi = lax.broadcasted_iota(jnp.int32, (T, 3 * T), 0)
    kj = lax.broadcasted_iota(jnp.int32, (T, 3 * T), 1)
    allowed = (kj <= qi + 2 * T) & (kj > qi + 2 * T - WINDOW_OF(T)) & (kj >= (2 - s) * T)
    bias[...] = jnp.where(allowed, 0.0, -1e30)
    allowed = (qi <= kj) & (qi > kj - WINDOW_OF(T)) & (kj < (NS - s) * T)
    bias_t[...] = jnp.where(allowed, 0.0, -1e30)

    pl.semaphore_wait(bar, (NX - 1) + 1 + (NY - 1) + (NZ - 1) + 4)

    plan = ((k_in, kw, 2 * T), (v_in, vw, 2 * T), (q_in, qw, 0), (g_in, gw, 0))

    def a2a_slices(i, ch, to):
        src, dst, first = plan[i]
        return (
            src.at[:, pl.ds(pl.multiple_of(to * WD + ch * CW, CW), CW)],
            dst.at[pl.ds(pl.multiple_of(first + x * RPD, RPD), RPD), pl.ds(ch * CW, CW)],
        )

    def a2a(i, ch, d):
        to = lax.rem(x + d, NX)
        return rc(*a2a_slices(i, ch, to), a2a_s.at[i, ch, d - 1], a2a_r.at[i, ch, d - 1], (s, to))

    def own_copy(i, ch):
        return pltpu.make_async_copy(*a2a_slices(i, ch, x), loc_sem.at[i, ch])

    for ch in range(CH):
        for i in range(4):
            for d in range(1, NX):
                a2a(i, ch, d).start()
            own_copy(i, ch).start()

    def a2a_wait(ch):
        for i in range(4):
            for d in range(1, NX):
                a2a(i, ch, d).wait_recv()
            own_copy(i, ch).wait()

    def far(i, ch):
        buf, first = plan[i][1], plan[i][2]
        cols = pl.ds(ch * CW, CW)
        return rc(
            buf.at[pl.ds(first, T), cols], buf.at[pl.ds(2 * T - first, T), cols],
            far_s.at[i, ch], far_r.at[i, ch], seq_off(2 if i < 2 else -2),
        )

    def near(i, ch):
        buf = plan[i][1]
        cols = pl.ds(ch * CW, CW)
        first = 2 * T * (1 - c)
        return rc(
            buf.at[pl.ds(pl.multiple_of(first, T), T), cols], buf.at[pl.ds(T, T), cols],
            near_s.at[i, ch], near_r.at[i, ch], at(z, y, 1 - c),
        )

    def send_near(ch, core, pair):
        @pl.when(c == core)
        def _():
            for i in pair:
                near(i, ch).start()

    def halo_start(ch):
        for i in range(4):
            far(i, ch).start()
        send_near(ch, 0, (0, 1))
        send_near(ch, 1, (2, 3))

    def halo_pass(ch):
        for i in range(4):
            far(i, ch).wait_recv()
        send_near(ch, 1, (0, 1))
        send_near(ch, 0, (2, 3))

    def c_copy(g, src, dst):
        return rc(src, dst, cl_s.at[g, 0], cl_r.at[g, 0], at(z, y, 1 - c))

    def y_copy(g, d, src, dst):
        return rc(src, dst, cl_s.at[g, d], cl_r.at[g, d], at(z, lax.rem(y + d, NY), c))

    def z_copy(g, d, src, dst):
        return rc(
            src, dst, cl_s.at[g, NY + d - 1], cl_r.at[g, NY + d - 1], at(lax.rem(z + d, NZ), y, c)
        )

    def z_loop(f):
        lax.fori_loop(1, NZ, lambda d, carry: (f(d), carry)[1], 0)

    cc0 = c_copy(0, cnt.at[0], cnt_c)
    cc0.start()
    cc0.wait()
    cnt[1] = cnt[0] + cnt_c[...]
    for d in range(1, NY):
        y_copy(0, d, cnt.at[1], cnt_y.at[d - 1]).start()
    total = cnt[1]
    for d in range(1, NY):
        y_copy(0, d, cnt.at[1], cnt_y.at[d - 1]).wait_recv()
        total = total + cnt_y[d - 1]
    cnt[2] = total
    z_loop(lambda d: z_copy(0, d, cnt.at[2], cnt_z.at[d - 1]).start())

    def head_cols(h):
        return pl.ds(pl.multiple_of(h * HD, HD), HD)

    own_rows = pl.ds(0, T)

    def add_sums(h, carry):
        m = mem[h]
        sums[h] = mm(m, qw[own_rows, head_cols(h)], NN)
        sums[H + h] = mm(m, gw[own_rows, head_cols(h)], NN)
        return carry

    for ch in range(CH):
        a2a_wait(ch)
        halo_start(ch)
        lax.fori_loop(ch * HPC, (ch + 1) * HPC, add_sums, 0)
        if ch > 1:
            halo_pass(ch - 2)
    my_half = pl.ds(pl.multiple_of(c * HC, HC), HC)
    their_half = pl.ds(pl.multiple_of((1 - c) * HC, HC), HC)
    cc1 = c_copy(1, sums.at[:, their_half, :], sums_c)
    cc1.start()
    cc1.wait_recv()

    def add_half(p, carry):
        v = sums[p, my_half, :] + sums_c[p]
        half[p] = v
        half_b[p] = v.astype(BF16)
        return carry

    lax.fori_loop(0, 2 * H, add_half, 0)

    def y_rows(yy):
        return pl.ds(pl.multiple_of(yy * ZR, ZR), ZR)

    def y1(d):
        return y_copy(1, d, half_b.at[:, y_rows(lax.rem(y + d, NY)), :], sums_y.at[d - 1])

    for d in range(1, NY):
        y1(d).start()

    for ch in range(max(CH - 2, 0), CH):
        halo_pass(ch)
    for d in range(1, NY):
        y1(d).wait_recv()
    for p in range(2 * H):
        v = half[p, y_rows(y), :]
        for d in range(1, NY):
            v = v + sums_y[d - 1, p].astype(F32)
        zs[pl.ds(p, NZ, stride=2 * H), :] = v

    def z1(d):
        to = lax.rem(z + d, NZ)
        rows = pl.ds(pl.multiple_of(to * 2 * H, 2 * H), 2 * H)
        return z_copy(1, d, zb.at[rows, :], zr.at[d - 1])

    zb[...] = zs[...].astype(BF16)
    z_loop(lambda d: z1(d).start())

    own_keys = pl.ds(2 * T, T)
    lanes_t = lax.broadcasted_iota(jnp.int32, (T, HD), 1)

    def query_side(h, carry):
        cols = head_cols(h)
        k, v = kw[:, cols], vw[:, cols]
        t = mm(qw[own_rows, cols], k, NT) * scale + bias[...]
        m = jnp.max(t, axis=1, keepdims=True)
        e = jnp.exp(t - m)
        rl = 1.0 / jnp.sum(e, axis=1, keepdims=True)
        p = e * rl
        wout[:, cols] = mm(p.astype(BF16), v, NN)
        dp = mm(gw[own_rows, cols], v, NT)
        delta = jnp.sum(p * dp, axis=1, keepdims=True)
        ds = (p * (dp - delta) * scale).astype(BF16)
        dq_out[:, cols] = mm(ds, k, NN).astype(BF16)
        old = jnp.where(lanes_t == h, m, sta[...])
        old = jnp.where(lanes_t == H + h, rl, old)
        sta[...] = jnp.where(lanes_t == 2 * H + h, delta, old)
        return carry

    def key_side(h, carry):
        cols = head_cols(h)
        q, g = qw[:, cols], gw[:, cols]
        t = mm(kw[own_keys, cols], q, NT) * scale + bias_t[...]
        p = jnp.exp(t - st[pl.ds(h, 1), :]) * st[pl.ds(H + h, 1), :]
        dp = mm(vw[own_keys, cols], g, NT)
        ds = (p * (dp - st[pl.ds(2 * H + h, 1), :]) * scale).astype(BF16)
        dkw[:, cols] = mm(ds, q, NN)
        dvw[:, cols] = mm(p.astype(BF16), g, NN)
        return carry

    def stat(o):
        return rc(
            st.at[:, pl.ds(0, T)], st.at[:, pl.ds(o * T, T)], st_s.at[o - 1], st_r.at[o - 1], seq_off(-o)
        )

    for ch in range(CH):
        for i in range(4):
            near(i, ch).wait_recv()

    sta[...] = jnp.zeros((T, HD), F32)
    early = H * 5 // 8
    lax.fori_loop(0, early, query_side, 0)
    z_loop(lambda d: z_copy(0, d, cnt.at[2], cnt_z.at[d - 1]).wait_recv())
    total = lax.fori_loop(0, NZ - 1, lambda d, t: t + cnt_z[d], cnt[2])
    count = pick(total, c * HC + y * ZR + z)

    z_loop(lambda d: z1(d).wait_recv())
    mine = lax.fori_loop(
        0, NZ - 1, lambda d, t: t + zr[d].astype(F32), zs[pl.ds(pl.multiple_of(z * 2 * H, 2 * H), 2 * H), :]
    )
    centroid = mine[0:H] / count
    cent_out[...] = centroid.astype(BF16)
    own[0:H, :] = centroid
    own[H : 2 * H, :] = mine[H:]
    agz[z] = own[...].astype(BF16)

    def z2(d):
        return z_copy(2, d, agz.at[z], agz.at[z])

    z_loop(lambda d: z2(d).start())
    lax.fori_loop(early, H, query_side, 0)
    st[:, 0:T] = jnp.transpose(sta[...])[0 : 3 * H]
    for o in (1, 2):
        stat(o).start()

    z_loop(lambda d: z2(d).wait_recv())
    for i in range(NZ):
        tmp[i * 2 * H : (i + 1) * 2 * H, :] = agz[i].astype(F32)
    for p in range(2 * H):
        hy[p] = tmp[pl.ds(p, NZ, stride=2 * H), :].astype(BF16)
    quarter = pl.ds(pl.multiple_of(c * HC + y * ZR, ZR), ZR)

    def y2(d):
        return y_copy(2, d, hy, cg.at[:, quarter, :])

    for d in range(1, NY):
        y2(d).start()
    cg[:, quarter, :] = hy[...]
    for d in range(1, NY):
        y2(d).wait_recv()
    cc2 = c_copy(2, cg.at[:, my_half, :], cg.at[:, my_half, :])
    cc2.start()
    cc2.wait_recv()

    lanes_c = lax.broadcasted_iota(jnp.int32, (C, HD), 1)
    tops, masses = jnp.zeros((C, HD), F32), jnp.zeros((C, HD), F32)
    for h in range(H):
        lg = mm(cg[h], kw[own_keys, head_cols(h)], NT) * scale
        lb[h] = lg
        m = jnp.max(lg, axis=1, keepdims=True)
        e = jnp.exp(lg - m)
        pay[h] = mm(e.astype(BF16), vw[own_keys, head_cols(h)], NN)
        tops = jnp.where(lanes_c == h, m, tops)
        masses = jnp.where(lanes_c == h, jnp.sum(e, axis=1, keepdims=True), masses)
    pay[H] = tops
    pay[H + 1] = masses
    cc3 = c_copy(3, pay.at[:, their_half, :], pay_c)
    cc3.start()

    cc3.wait_recv()
    ma, mb = pay[H, my_half, :], pay_c[H]
    mm_ = jnp.maximum(ma, mb)
    fa, fb = jnp.exp(ma - mm_), jnp.exp(mb - mm_)
    mass = pay[H + 1, my_half, :] * fa + pay_c[H + 1] * fb
    pay_h[H] = mm_
    pay_h[H + 1] = mass
    for n, v in enumerate(split(mm_) + split(mass)):
        pay_b[H + n] = v
    for h in range(H):
        v = pay[h, my_half, :] * fa[:, h : h + 1] + pay_c[h] * fb[:, h : h + 1]
        pay_h[h] = v
        pay_b[h] = v.astype(BF16)

    def y3(d):
        return y_copy(3, d, pay_b.at[:, y_rows(lax.rem(y + d, NY)), :], pay_y.at[d - 1])

    for d in range(1, NY):
        y3(d).start()

    for d in range(1, NY):
        y3(d).wait_recv()
    ms = [pay_h[H, y_rows(y), :]] + [join([pay_y[d, H + n] for n in range(3)]) for d in range(NY - 1)]
    ls = [pay_h[H + 1, y_rows(y), :]] + [
        join([pay_y[d, H + 3 + n] for n in range(3)]) for d in range(NY - 1)
    ]
    top = functools.reduce(jnp.maximum, ms)
    fs = [jnp.exp(m - top) for m in ms]
    for h in range(H):
        v = pay_h[h, y_rows(y), :] * fs[0][:, h : h + 1]
        for d in range(NY - 1):
            v = v + pay_y[d, h].astype(F32) * fs[d + 1][:, h : h + 1]
        zs2[pl.ds(h, NZ, stride=16), :] = v
    mass = functools.reduce(lambda a, b: a + b, [a * b for a, b in zip(ls, fs)])
    for n, v in enumerate(split(top) + split(mass)):
        zs2[pl.ds(H + n, NZ, stride=16), :] = v.astype(F32)
    for p in range(H + 6, 16):
        zs2[pl.ds(p, NZ, stride=16), :] = jnp.zeros((NZ, HD), F32)
    zb2[...] = zs2[...].astype(BF16)

    def z3(d):
        to = lax.rem(z + d, NZ)
        rows = pl.ds(pl.multiple_of(to * 16, 16), 16)
        return z_copy(3, d, zb2.at[rows, :], zr2.at[pl.ds(pl.multiple_of(d * 16, 16), 16), :])

    z_loop(lambda d: z3(d).start())
    zr2[0:16, :] = zb2[pl.ds(pl.multiple_of(z * 16, 16), 16), :]

    for o in (1, 2):
        stat(o).wait_recv()
    lax.fori_loop(0, H, key_side, 0)
    z_loop(lambda d: z3(d).wait_recv())
    tmp[0 : NZ * 16, :] = zr2[...].astype(F32)
    mz = join([tmp[pl.ds(H + n, NZ, stride=16), :] for n in range(3)])
    lz = join([tmp[pl.ds(H + 3 + n, NZ, stride=16), :] for n in range(3)])
    topz = jnp.max(mz, axis=0, keepdims=True)
    fz = jnp.exp(mz - topz)
    lrow = jnp.sum(lz * fz, axis=0, keepdims=True)
    diag = lax.broadcasted_iota(jnp.int32, (H, HD), 0) == lax.broadcasted_iota(
        jnp.int32, (H, HD), 1
    )

    def column(row):
        return jnp.sum(jnp.where(diag, row, 0.0), axis=1, keepdims=True)

    acc = jnp.zeros((H, HD), F32)
    for i in range(NZ):
        acc = acc + tmp[i * 16 : i * 16 + H, :] * column(fz[i : i + 1, :])
    c_out = acc / column(lrow)
    grad = own[H : 2 * H, :].astype(BF16).astype(F32)
    c_delta = jnp.sum(grad * c_out, axis=1, keepdims=True)
    tmp[0:16, :] = jnp.zeros((16, HD), F32)
    tmp[0:H, :] = c_out
    delta_row = jnp.sum(jnp.where(diag, c_delta, 0.0), axis=0, keepdims=True)
    for n, v in enumerate(split(topz + jnp.log(jnp.where(lrow > 0.0, lrow, 1.0))) + split(delta_row)):
        tmp[H + n : H + n + 1, :] = v.astype(F32)
    blk[...] = tmp[0:16, :].astype(BF16)

    my_rows16 = pl.ds(pl.multiple_of(z * 16, 16), 16)

    def z4(d):
        return z_copy(4, d, blk, agz2.at[my_rows16, :])

    z_loop(lambda d: z4(d).start())
    agz2[my_rows16, :] = blk[...]
    z_loop(lambda d: z4(d).wait_recv())
    tmp[0 : NZ * 16, :] = agz2[...].astype(F32)
    for p in range(H + 6):
        co[p, quarter, :] = tmp[pl.ds(p, NZ, stride=16), :].astype(BF16)

    def y4(d):
        return y_copy(4, d, co.at[:, quarter, :], co.at[:, quarter, :])

    for d in range(1, NY):
        y4(d).start()
    for d in range(1, NY):
        y4(d).wait_recv()
    cc4 = c_copy(4, co.at[:, my_half, :], co.at[:, my_half, :])
    cc4.start()
    cc4.wait_recv()

    lse = join([co[H + n] for n in range(3)])
    deltas = join([co[H + 3 + n] for n in range(3)])
    for h in range(H):
        cols = head_cols(h)
        w = jnp.exp(lb[h] - pick(lse, h))
        dw = mm(cg[H + h], vw[own_keys, cols], NT)
        dl = (w * (dw - pick(deltas, h)) * scale).astype(BF16)
        attn_out[:, cols] = (wout[:, cols] + mm(mem[h], co[h], TN)).astype(BF16)
        dk_out[:, cols] = (dkw[:, cols] + mm(dl, cg[h], TN)).astype(BF16)
        dv_out[:, cols] = (dvw[:, cols] + mm(w.astype(BF16), cg[H + h], TN)).astype(BF16)

    for ch in range(CH):
        for i in range(4):
            for d in range(1, NX):
                a2a(i, ch, d).wait_send()
            far(i, ch).wait_send()
            near(i, ch).wait_send()
    for o in (1, 2):
        stat(o).wait_send()
    for cp in (cc1, cc2, cc3, cc4):
        cp.wait_send()
    for d in range(1, NY):
        y_copy(0, d, cnt.at[1], cnt_y.at[d - 1]).wait_send()
        y1(d).wait_send()
        y2(d).wait_send()
        y3(d).wait_send()
        y4(d).wait_send()

    def drain(d):
        z_copy(0, d, cnt.at[2], cnt_z.at[d - 1]).wait_send()
        z1(d).wait_send()
        z2(d).wait_send()
        z3(d).wait_send()
        z4(d).wait_send()

    z_loop(drain)


def WINDOW_OF(tokens):
    return WINDOW if tokens == 256 else 2 * tokens


def solution(mesh):
    NX = mesh.shape["head"]
    NZ, NY, NC = factors(mesh.shape["seq"])
    HD, CH = HEAD_DIM, 4

    def body(q, k, v, g, clusters, owner_slot):
        H, T = clusters.shape
        C = owner_slot.shape[1]
        WD = H * HD
        HC, ZR = C // NC, NZ
        dims = (NX, NZ, NY, NC, H, T, HD, CH)
        V, D = pltpu.VMEM, pltpu.SemaphoreType.DMA
        groups = 5
        scratch = [
            V((3 * T, WD), BF16), V((3 * T, WD), BF16), V((3 * T, WD), BF16), V((3 * T, WD), BF16),
            V((T, WD), F32), V((T, WD), F32), V((H, C, T), BF16),
            V((T, WD), F32), V((T, 3 * T), F32), V((T, 3 * T), F32), V((T, HD), F32),
            V((3 * H, 3 * T), F32),
            V((3, H, C), F32), V((H, C), F32), V((NY - 1, H, C), F32), V((NZ - 1, H, C), F32),
            V((2 * H, C, HD), F32), V((2 * H, HC, HD), F32), V((2 * H, HC, HD), F32),
            V((2 * H, HC, HD), BF16), V((NY - 1, 2 * H, ZR, HD), BF16), V((NZ * 2 * H, HD), F32),
            V((NZ * 2 * H, HD), BF16), V((NZ - 1, 2 * H, HD), BF16), V((2 * H, HD), F32),
            V((NZ, 2 * H, HD), BF16), V((NZ * 16, HD), F32), V((2 * H, NZ, HD), BF16),
            V((2 * H, C, HD), BF16),
            V((H, C, T), F32), V((H + 2, C, HD), F32), V((H + 2, HC, HD), F32),
            V((H + 2, HC, HD), F32), V((H + 6, HC, HD), BF16), V((NY - 1, H + 6, ZR, HD), BF16),
            V((NZ * 16, HD), F32), V((NZ * 16, HD), BF16), V((NZ * 16, HD), BF16),
            V((16, HD), BF16), V((NZ * 16, HD), BF16), V((H + 6, C, HD), BF16),
            D((4, CH)), D((4, CH, NX - 1)), D((4, CH, NX - 1)), D((4, CH)), D((4, CH)),
            D((4, CH)), D((4, CH)), D((2,)), D((2,)), D((groups, NY + NZ - 1)), D((groups, NY + NZ - 1)),
        ]
        wide = jax.ShapeDtypeStruct((T, WD), BF16)
        hbm = pl.BlockSpec(memory_space=pl.ANY)
        vmem = pl.BlockSpec(memory_space=pltpu.VMEM)
        outs = pl.pallas_call(
            functools.partial(kernel, dims),
            out_shape=(wide, wide, wide, wide, jax.ShapeDtypeStruct((H, HD), BF16)),
            in_specs=[hbm] * 4 + [vmem] * 2,
            out_specs=(vmem,) * 5,
            scratch_shapes=scratch,
            compiler_params=pltpu.CompilerParams(
                collective_id=0, has_side_effects=True, vmem_limit_bytes=60 * 1024 * 1024
            ),
        )(q, k, v, g, clusters, owner_slot)
        return (*outs[:4], outs[4].reshape(H, 1, HD))

    rows = P(("seq", "head"), None)
    return jax.shard_map(
        body,
        mesh=mesh,
        in_specs=(rows, rows, rows, rows, P("head", "seq"), P("head", None)),
        out_specs=(P("seq", "head"),) * 4 + (P("head", "seq", None),),
        check_vma=False,
    )
```

```python
import functools

import jax
import jax.numpy as jnp
from jax import lax
from jax.experimental import pallas as pl
from jax.experimental.pallas import tpu as pltpu
from jax.sharding import PartitionSpec as P

HEAD_DIM = 128
WINDOW = 512
F32 = jnp.float32
BF16 = jnp.bfloat16
NN = (((1,), (0,)), ((), ()))
NT = (((1,), (1,)), ((), ()))
TN = (((0,), (0,)), ((), ()))


def factors(count):
    return {128: (16, 4, 2), 8: (2, 2, 2)}[count]


def mm(a, b, dims):
    return lax.dot_general(a, b, dims, preferred_element_type=F32)


def split(v):
    hi = v.astype(BF16)
    rest = v - hi.astype(F32)
    mid = rest.astype(BF16)
    return hi, mid, (rest - mid.astype(F32)).astype(BF16)


def join(parts):
    return functools.reduce(lambda a, b: a + b, [p.astype(F32) for p in parts])


def pick(table, lane):
    lanes = lax.broadcasted_iota(jnp.int32, table.shape, 1)
    return jnp.sum(jnp.where(lanes == lane, table, 0.0), axis=1, keepdims=True)


def kernel(
    dims, q_in, k_in, v_in, g_in, clus_in, slot_in, attn_out, dq_out, dk_out, dv_out, cent_out,
    qw, gw, kw, vw, dkw, dvw, mem, wout, bias, bias_t, sta, st,
    cnt, cnt_c, cnt_y, cnt_z,
    sums, sums_c, half, half_b, sums_y, zs, zb, zr, own,
    agz, tmp, hy, cg,
    lb, pay, pay_c, pay_h, pay_b, pay_y, zs2, zb2, zr2,
    blk, agz2, co, clus, slot,
    loc_sem, a2a_s, a2a_r, far_s, far_r, near_s, near_r, st_s, st_r, cl_s, cl_r, co_s, co_r, ids_sem,
):
    NX, NZ, NY, NC, H, T, HD, CH = dims
    NS = NZ * NY * NC
    C = NS
    RPD = T // NX
    HC = C // NC
    ZR = NZ
    HPC = H // CH
    CW = HPC * HD
    WD = H * HD
    scale = HEAD_DIM ** (-0.5)
    s = lax.axis_index("seq")
    x = lax.axis_index("head")
    c = lax.rem(s, NC)
    y = lax.rem(lax.div(s, NC), NY)
    z = lax.div(s, NC * NY)

    def at(zz, yy, cc):
        return ((zz * NY + yy) * NC + cc, x)

    def seq_off(k):
        return (lax.rem(s + k + NS, NS), x)

    def rc(src, dst, ss, rs, dev):
        return pltpu.make_async_remote_copy(
            src_ref=src, dst_ref=dst, send_sem=ss, recv_sem=rs, device_id=dev,
            device_id_type=pl.DeviceIdType.MESH,
        )

    ids = (
        pltpu.make_async_copy(clus_in, clus, ids_sem.at[0]),
        pltpu.make_async_copy(slot_in, slot, ids_sem.at[1]),
    )
    for cp in ids:
        cp.start()
    bar = pltpu.get_barrier_semaphore()

    def hello(dev):
        pl.semaphore_signal(bar, inc=1, device_id=dev, device_id_type=pl.DeviceIdType.MESH)

    for d in range(1, NX):
        hello((s, lax.rem(x + d, NX)))
    hello(at(z, y, 1 - c))
    for d in range(1, NY):
        hello(at(z, lax.rem(y + d, NY), c))

    def hello_z(d, carry):
        hello(at(lax.rem(z + d, NZ), y, c))
        return carry

    lax.fori_loop(1, NZ, hello_z, 0)
    for k in (-2, -1, 1, 2):
        hello(seq_off(k))

    pl.semaphore_wait(bar, (NX - 1) + 1 + (NY - 1) + (NZ - 1) + 4)

    plan = ((k_in, kw, 2 * T), (v_in, vw, 2 * T), (q_in, qw, 0), (g_in, gw, 0))

    def a2a_slices(i, ch, to):
        src, dst, first = plan[i]
        return (
            src.at[:, pl.ds(pl.multiple_of(to * WD + ch * CW, CW), CW)],
            dst.at[pl.ds(pl.multiple_of(first + x * RPD, RPD), RPD), pl.ds(ch * CW, CW)],
        )

    def a2a(i, ch, d):
        to = lax.rem(x + d, NX)
        return rc(*a2a_slices(i, ch, to), a2a_s.at[i, ch, d - 1], a2a_r.at[i, ch, d - 1], (s, to))

    def own_copy(i, ch):
        return pltpu.make_async_copy(*a2a_slices(i, ch, x), loc_sem.at[i, ch])

    for ch in range(CH):
        for i in range(4):
            for d in range(1, NX):
                a2a(i, ch, d).start()
            own_copy(i, ch).start()

    def a2a_wait(ch):
        for i in range(4):
            for d in range(1, NX):
                a2a(i, ch, d).wait_recv()
            own_copy(i, ch).wait()

    def far(i, ch):
        buf, first = plan[i][1], plan[i][2]
        cols = pl.ds(ch * CW, CW)
        return rc(
            buf.at[pl.ds(first, T), cols], buf.at[pl.ds(2 * T - first, T), cols],
            far_s.at[i, ch], far_r.at[i, ch], seq_off(2 if i < 2 else -2),
        )

    def near(i, ch):
        buf = plan[i][1]
        cols = pl.ds(ch * CW, CW)
        first = 2 * T * (1 - c)
        return rc(
            buf.at[pl.ds(pl.multiple_of(first, T), T), cols], buf.at[pl.ds(T, T), cols],
            near_s.at[i, ch], near_r.at[i, ch], at(z, y, 1 - c),
        )

    def send_near(ch, core, pair):
        @pl.when(c == core)
        def _():
            for i in pair:
                near(i, ch).start()

    def halo_start(ch):
        for i in range(4):
            far(i, ch).start()
        send_near(ch, 0, (0, 1))
        send_near(ch, 1, (2, 3))

    def halo_pass(ch):
        for i in range(4):
            far(i, ch).wait_recv()
        send_near(ch, 1, (0, 1))
        send_near(ch, 0, (2, 3))

    for cp in ids:
        cp.wait()
    row_ids = lax.broadcasted_iota(jnp.int32, (C, C), 0)
    clu_ids = lax.broadcasted_iota(jnp.int32, (C, T), 0)

    def members(h, carry):
        r = slot[pl.ds(h, 1), :]
        ps = lax.rem(r, NC) * (NY * NZ) + lax.rem(lax.div(r, NC), NY) * NZ + lax.div(r, NC * NY)
        slot_pick = jnp.where(ps == row_ids, 1.0, 0.0).astype(BF16)
        clu_pick = jnp.where(clus[pl.ds(h, 1), :] == clu_ids, 1.0, 0.0).astype(BF16)
        m = mm(slot_pick, clu_pick, NN).astype(BF16)
        mem[h] = m
        cnt[0, pl.ds(h, 1), :] = mm(jnp.ones((8, T), BF16), m, NT)[0:1]
        return carry

    lax.fori_loop(0, H, members, 0)
    qi = lax.broadcasted_iota(jnp.int32, (T, 3 * T), 0)
    kj = lax.broadcasted_iota(jnp.int32, (T, 3 * T), 1)
    allowed = (kj <= qi + 2 * T) & (kj > qi + 2 * T - WINDOW_OF(T)) & (kj >= (2 - s) * T)
    bias[...] = jnp.where(allowed, 0.0, -1e30)
    allowed = (qi <= kj) & (qi > kj - WINDOW_OF(T)) & (kj < (NS - s) * T)
    bias_t[...] = jnp.where(allowed, 0.0, -1e30)

    def c_copy(g, src, dst):
        return rc(src, dst, cl_s.at[g, 0], cl_r.at[g, 0], at(z, y, 1 - c))

    def y_copy(g, d, src, dst):
        return rc(src, dst, cl_s.at[g, d], cl_r.at[g, d], at(z, lax.rem(y + d, NY), c))

    def z_copy(g, d, src, dst):
        return rc(
            src, dst, cl_s.at[g, NY + d - 1], cl_r.at[g, NY + d - 1], at(lax.rem(z + d, NZ), y, c)
        )

    def z_loop(f):
        lax.fori_loop(1, NZ, lambda d, carry: (f(d), carry)[1], 0)

    def q_copy(g, d, src, dst):
        return rc(src, dst, co_s.at[g, d], co_r.at[g, d], at(z, y, 1 - c))

    near_first = sorted(range(1, NY), key=lambda d: (min(d, NY - d), d))
    far_first = near_first[::-1]

    cc0 = c_copy(0, cnt.at[0], cnt_c)
    cc0.start()
    cc0.wait()
    cnt[1] = cnt[0] + cnt_c[...]
    for d in range(1, NY):
        y_copy(0, d, cnt.at[1], cnt_y.at[d - 1]).start()
    total = cnt[1]
    for d in range(1, NY):
        y_copy(0, d, cnt.at[1], cnt_y.at[d - 1]).wait_recv()
        total = total + cnt_y[d - 1]
    cnt[2] = total
    z_loop(lambda d: z_copy(0, d, cnt.at[2], cnt_z.at[d - 1]).start())

    def head_cols(h):
        return pl.ds(pl.multiple_of(h * HD, HD), HD)

    own_rows = pl.ds(0, T)

    def add_sums(h, carry):
        m = mem[h]
        sums[h] = mm(m, qw[own_rows, head_cols(h)], NN)
        sums[H + h] = mm(m, gw[own_rows, head_cols(h)], NN)
        return carry

    for ch in range(CH):
        a2a_wait(ch)
        if ch < CH - 1:
            halo_start(ch)
        lax.fori_loop(ch * HPC, (ch + 1) * HPC, add_sums, 0)
        if ch > 1:
            halo_pass(ch - 2)
    my_half = pl.ds(pl.multiple_of(c * HC, HC), HC)
    their_half = pl.ds(pl.multiple_of((1 - c) * HC, HC), HC)
    def half_rows(core, yy):
        return pl.ds(pl.multiple_of(core * HC + yy * ZR, ZR), ZR)

    def y_rows(yy):
        return pl.ds(pl.multiple_of(yy * ZR, ZR), ZR)

    def up(d):
        return lax.rem(y + d, NY)

    def down(d):
        return lax.rem(y - d + NY, NY)

    def c1(d):
        return q_copy(0, d, sums.at[:, half_rows(1 - c, up(d)), :], sums_c.at[:, y_rows(up(d)), :])

    def y1(d):
        return y_copy(1, d, half_b.at[:, y_rows(up(d)), :], sums_y.at[d - 1])

    for d in far_first + [0]:
        c1(d).start()
    for d in far_first + [0]:
        c1(d).wait_recv()
        v = sums[:, half_rows(c, up(d)), :] + sums_c[:, y_rows(up(d)), :]
        if d:
            half_b[:, y_rows(up(d)), :] = v.astype(BF16)
            y1(d).start()
        else:
            half[:, y_rows(y), :] = v
    for d in range(1, NY):
        y1(d).wait_recv()
    for p in range(2 * H):
        v = half[p, y_rows(y), :]
        for d in range(1, NY):
            v = v + sums_y[d - 1, p].astype(F32)
        zs[pl.ds(p, NZ, stride=2 * H), :] = v

    def z1(d):
        to = lax.rem(z + d, NZ)
        rows = pl.ds(pl.multiple_of(to * 2 * H, 2 * H), 2 * H)
        return z_copy(1, d, zb.at[rows, :], zr.at[d - 1])

    zb[...] = zs[...].astype(BF16)
    z_loop(lambda d: z1(d).start())
    halo_start(CH - 1)

    own_keys = pl.ds(2 * T, T)
    lanes_t = lax.broadcasted_iota(jnp.int32, (T, HD), 1)

    def query_side(h, carry):
        cols = head_cols(h)
        k, v = kw[:, cols], vw[:, cols]
        t = mm(qw[own_rows, cols], k, NT) * scale + bias[...]
        m = jnp.max(t, axis=1, keepdims=True)
        e = jnp.exp(t - m)
        rl = 1.0 / jnp.sum(e, axis=1, keepdims=True)
        p = e * rl
        wout[:, cols] = mm(p.astype(BF16), v, NN)
        dp = mm(gw[own_rows, cols], v, NT)
        delta = jnp.sum(p * dp, axis=1, keepdims=True)
        ds = (p * (dp - delta) * scale).astype(BF16)
        dq_out[:, cols] = mm(ds, k, NN).astype(BF16)
        old = jnp.where(lanes_t == h, m, sta[...])
        old = jnp.where(lanes_t == H + h, rl, old)
        sta[...] = jnp.where(lanes_t == 2 * H + h, delta, old)
        return carry

    def key_side(h, carry):
        cols = head_cols(h)
        q, g = qw[:, cols], gw[:, cols]
        t = mm(kw[own_keys, cols], q, NT) * scale + bias_t[...]
        p = jnp.exp(t - st[pl.ds(h, 1), :]) * st[pl.ds(H + h, 1), :]
        dp = mm(vw[own_keys, cols], g, NT)
        ds = (p * (dp - st[pl.ds(2 * H + h, 1), :]) * scale).astype(BF16)
        dkw[:, cols] = mm(ds, q, NN)
        dvw[:, cols] = mm(p.astype(BF16), g, NN)
        return carry

    def stat(o):
        return rc(
            st.at[:, pl.ds(0, T)], st.at[:, pl.ds(o * T, T)], st_s.at[o - 1], st_r.at[o - 1], seq_off(-o)
        )

    for ch in range(CH - 2):
        for i in range(4):
            near(i, ch).wait_recv()

    sta[...] = jnp.zeros((T, HD), F32)
    lax.fori_loop(0, (CH - 2) * HPC, query_side, 0)
    halo_pass(CH - 2)
    z_loop(lambda d: z_copy(0, d, cnt.at[2], cnt_z.at[d - 1]).wait_recv())
    total = lax.fori_loop(0, NZ - 1, lambda d, t: t + cnt_z[d], cnt[2])
    count = pick(total, c * HC + y * ZR + z)

    z_loop(lambda d: z1(d).wait_recv())
    mine = lax.fori_loop(
        0, NZ - 1, lambda d, t: t + zr[d].astype(F32), zs[pl.ds(pl.multiple_of(z * 2 * H, 2 * H), 2 * H), :]
    )
    centroid = mine[0:H] / count
    cent_out[...] = centroid.astype(BF16)
    own[0:H, :] = centroid
    own[H : 2 * H, :] = mine[H:]
    agz[z] = own[...].astype(BF16)

    def z2(d):
        return z_copy(2, d, agz.at[z], agz.at[z])

    z_loop(lambda d: z2(d).start())
    for i in range(4):
        near(i, CH - 2).wait_recv()
    lax.fori_loop((CH - 2) * HPC, (CH - 1) * HPC, query_side, 0)
    halo_pass(CH - 1)
    z_loop(lambda d: z2(d).wait_recv())
    for i in range(NZ):
        tmp[i * 2 * H : (i + 1) * 2 * H, :] = agz[i].astype(F32)
    for p in range(2 * H):
        hy[p] = tmp[pl.ds(p, NZ, stride=2 * H), :].astype(BF16)
    quarter = half_rows(c, y)
    sides = (pl.ds(0, H), pl.ds(H, H))

    def y2(side, d):
        return y_copy(2 + 3 * side, d, hy.at[sides[side]], cg.at[sides[side], quarter, :])

    def c2(side, d):
        where = cg.at[sides[side], half_rows(c, down(d)), :]
        return q_copy(1 + side, d, hy.at[sides[side]] if d == 0 else where, where)

    for side in range(2):
        for d in far_first:
            y2(side, d).start()
    c2(0, 0).start()
    cg[:, quarter, :] = hy[...]
    for i in range(4):
        near(i, CH - 1).wait_recv()
    lax.fori_loop((CH - 1) * HPC, H, query_side, 0)
    st[:, 0:T] = jnp.transpose(sta[...])[0 : 3 * H]
    for o in (1, 2):
        stat(o).start()

    for d in near_first:
        y2(0, d).wait_recv()
        c2(0, d).start()
    for d in range(NY):
        c2(0, d).wait_recv()

    lanes_c = lax.broadcasted_iota(jnp.int32, (C, HD), 1)
    tops, masses = jnp.zeros((C, HD), F32), jnp.zeros((C, HD), F32)
    for h in range(H):
        lg = mm(cg[h], kw[own_keys, head_cols(h)], NT) * scale
        lb[h] = lg
        m = jnp.max(lg, axis=1, keepdims=True)
        e = jnp.exp(lg - m)
        pay[h] = mm(e.astype(BF16), vw[own_keys, head_cols(h)], NN)
        tops = jnp.where(lanes_c == h, m, tops)
        masses = jnp.where(lanes_c == h, jnp.sum(e, axis=1, keepdims=True), masses)
    pay[H] = tops
    pay[H + 1] = masses
    def c3(d):
        return q_copy(3, d, pay.at[:, half_rows(1 - c, up(d)), :], pay_c.at[:, y_rows(up(d)), :])

    def y3(d):
        return y_copy(3, d, pay_b.at[:, y_rows(up(d)), :], pay_y.at[d - 1])

    for d in far_first + [0]:
        c3(d).start()
    c2(1, 0).start()
    for d in near_first:
        y2(1, d).wait_recv()
        c2(1, d).start()
    for d in far_first + [0]:
        c3(d).wait_recv()
        mine_q, rows = half_rows(c, up(d)), y_rows(up(d))
        ma, mb = pay[H, mine_q, :], pay_c[H, rows, :]
        top = jnp.maximum(ma, mb)
        fa, fb = jnp.exp(ma - top), jnp.exp(mb - top)
        mass = pay[H + 1, mine_q, :] * fa + pay_c[H + 1, rows, :] * fb
        if d:
            for n, v in enumerate(split(top) + split(mass)):
                pay_b[H + n, rows, :] = v
        else:
            pay_h[H, rows, :] = top
            pay_h[H + 1, rows, :] = mass
        for h in range(H):
            v = pay[h, mine_q, :] * fa[:, h : h + 1] + pay_c[h, rows, :] * fb[:, h : h + 1]
            if d:
                pay_b[h, rows, :] = v.astype(BF16)
            else:
                pay_h[h, rows, :] = v
        if d:
            y3(d).start()

    for o in (1, 2):
        stat(o).wait_recv()
    some = H * 3 // 8
    lax.fori_loop(0, some, key_side, 0)
    for d in range(1, NY):
        y3(d).wait_recv()
    ms = [pay_h[H, y_rows(y), :]] + [join([pay_y[d, H + n] for n in range(3)]) for d in range(NY - 1)]
    ls = [pay_h[H + 1, y_rows(y), :]] + [
        join([pay_y[d, H + 3 + n] for n in range(3)]) for d in range(NY - 1)
    ]
    top = functools.reduce(jnp.maximum, ms)
    fs = [jnp.exp(m - top) for m in ms]
    for h in range(H):
        v = pay_h[h, y_rows(y), :] * fs[0][:, h : h + 1]
        for d in range(NY - 1):
            v = v + pay_y[d, h].astype(F32) * fs[d + 1][:, h : h + 1]
        zs2[pl.ds(h, NZ, stride=16), :] = v
    mass = functools.reduce(lambda a, b: a + b, [a * b for a, b in zip(ls, fs)])
    for n, v in enumerate(split(top) + split(mass)):
        zs2[pl.ds(H + n, NZ, stride=16), :] = v.astype(F32)
    for p in range(H + 6, 16):
        zs2[pl.ds(p, NZ, stride=16), :] = jnp.zeros((NZ, HD), F32)
    zb2[...] = zs2[...].astype(BF16)

    def z3(d):
        to = lax.rem(z + d, NZ)
        rows = pl.ds(pl.multiple_of(to * 16, 16), 16)
        return z_copy(3, d, zb2.at[rows, :], zr2.at[pl.ds(pl.multiple_of(d * 16, 16), 16), :])

    z_loop(lambda d: z3(d).start())
    zr2[0:16, :] = zb2[pl.ds(pl.multiple_of(z * 16, 16), 16), :]

    lax.fori_loop(some, H, key_side, 0)
    z_loop(lambda d: z3(d).wait_recv())
    tmp[0 : NZ * 16, :] = zr2[...].astype(F32)
    mz = join([tmp[pl.ds(H + n, NZ, stride=16), :] for n in range(3)])
    lz = join([tmp[pl.ds(H + 3 + n, NZ, stride=16), :] for n in range(3)])
    topz = jnp.max(mz, axis=0, keepdims=True)
    fz = jnp.exp(mz - topz)
    lrow = jnp.sum(lz * fz, axis=0, keepdims=True)
    diag = lax.broadcasted_iota(jnp.int32, (H, HD), 0) == lax.broadcasted_iota(
        jnp.int32, (H, HD), 1
    )

    def column(row):
        return jnp.sum(jnp.where(diag, row, 0.0), axis=1, keepdims=True)

    acc = jnp.zeros((H, HD), F32)
    for i in range(NZ):
        acc = acc + tmp[i * 16 : i * 16 + H, :] * column(fz[i : i + 1, :])
    c_out = acc / column(lrow)
    grad = own[H : 2 * H, :].astype(BF16).astype(F32)
    c_delta = jnp.sum(grad * c_out, axis=1, keepdims=True)
    tmp[0:16, :] = jnp.zeros((16, HD), F32)
    tmp[0:H, :] = c_out
    delta_row = jnp.sum(jnp.where(diag, c_delta, 0.0), axis=0, keepdims=True)
    for n, v in enumerate(split(topz + jnp.log(jnp.where(lrow > 0.0, lrow, 1.0))) + split(delta_row)):
        tmp[H + n : H + n + 1, :] = v.astype(F32)
    blk[...] = tmp[0:16, :].astype(BF16)

    my_rows16 = pl.ds(pl.multiple_of(z * 16, 16), 16)

    def z4(d):
        return z_copy(4, d, blk, agz2.at[my_rows16, :])

    z_loop(lambda d: z4(d).start())
    agz2[my_rows16, :] = blk[...]
    for ch in range(CH):
        for i in range(4):
            for d in range(1, NX):
                a2a(i, ch, d).wait_send()
            far(i, ch).wait_send()
            near(i, ch).wait_send()
    for o in (1, 2):
        stat(o).wait_send()
    for d in range(1, NY):
        y_copy(0, d, cnt.at[1], cnt_y.at[d - 1]).wait_send()
        for cp in (y1(d), y2(0, d), y2(1, d), y3(d)):
            cp.wait_send()
    for d in range(NY):
        for cp in (c1(d), c2(0, d), c2(1, d), c3(d)):
            cp.wait_send()

    def drain(d):
        z_copy(0, d, cnt.at[2], cnt_z.at[d - 1]).wait_send()
        z1(d).wait_send()
        z2(d).wait_send()
        z3(d).wait_send()

    z_loop(drain)
    z_loop(lambda d: z4(d).wait())
    tmp[0 : NZ * 16, :] = agz2[...].astype(F32)
    for p in range(H + 6):
        co[p, quarter, :] = tmp[pl.ds(p, NZ, stride=16), :].astype(BF16)

    def y4(d):
        return y_copy(4, d, co.at[:, quarter, :], co.at[:, quarter, :])

    def c4(d):
        where = co.at[:, half_rows(c, down(d)), :]
        return q_copy(4, d, where, where)

    for d in far_first:
        y4(d).start()
    c4(0).start()
    for d in near_first:
        y4(d).wait_recv()
        c4(d).start()
    for d in range(NY):
        c2(1, d).wait_recv()
    for d in range(NY):
        c4(d).wait_recv()

    lse = join([co[H + n] for n in range(3)])
    deltas = join([co[H + 3 + n] for n in range(3)])
    for h in range(H):
        cols = head_cols(h)
        w = jnp.exp(lb[h] - pick(lse, h))
        dw = mm(cg[H + h], vw[own_keys, cols], NT)
        dl = (w * (dw - pick(deltas, h)) * scale).astype(BF16)
        attn_out[:, cols] = (wout[:, cols] + mm(mem[h], co[h], TN)).astype(BF16)
        dk_out[:, cols] = (dkw[:, cols] + mm(dl, cg[h], TN)).astype(BF16)
        dv_out[:, cols] = (dvw[:, cols] + mm(w.astype(BF16), cg[H + h], TN)).astype(BF16)

    for d in range(1, NY):
        y4(d).wait_send()
    for d in range(NY):
        c4(d).wait_send()


def flush(*refs):
    sem = refs[10]
    copies = [pltpu.make_async_copy(refs[i], refs[5 + i], sem.at[i]) for i in range(5)]
    for cp in copies:
        cp.start()
    for cp in copies:
        cp.wait()


def WINDOW_OF(tokens):
    return WINDOW if tokens == 256 else 2 * tokens


def solution(mesh):
    NX = mesh.shape["head"]
    NZ, NY, NC = factors(mesh.shape["seq"])
    HD, CH = HEAD_DIM, 4

    def body(q, k, v, g, clusters, owner_slot):
        H, T = clusters.shape
        C = owner_slot.shape[1]
        WD = H * HD
        HC, ZR = C // NC, NZ
        dims = (NX, NZ, NY, NC, H, T, HD, CH)
        V, D = pltpu.VMEM, pltpu.SemaphoreType.DMA
        groups = 6
        scratch = [
            V((3 * T, WD), BF16), V((3 * T, WD), BF16), V((3 * T, WD), BF16), V((3 * T, WD), BF16),
            V((T, WD), F32), V((T, WD), F32), V((H, C, T), BF16),
            V((T, WD), F32), V((T, 3 * T), F32), V((T, 3 * T), F32), V((T, HD), F32),
            V((3 * H, 3 * T), F32),
            V((3, H, C), F32), V((H, C), F32), V((NY - 1, H, C), F32), V((NZ - 1, H, C), F32),
            V((2 * H, C, HD), F32), V((2 * H, HC, HD), F32), V((2 * H, HC, HD), F32),
            V((2 * H, HC, HD), BF16), V((NY - 1, 2 * H, ZR, HD), BF16), V((NZ * 2 * H, HD), F32),
            V((NZ * 2 * H, HD), BF16), V((NZ - 1, 2 * H, HD), BF16), V((2 * H, HD), F32),
            V((NZ, 2 * H, HD), BF16), V((NZ * 16, HD), F32), V((2 * H, NZ, HD), BF16),
            V((2 * H, C, HD), BF16),
            V((H, C, T), F32), V((H + 2, C, HD), F32), V((H + 2, HC, HD), F32),
            V((H + 2, HC, HD), F32), V((H + 6, HC, HD), BF16), V((NY - 1, H + 6, ZR, HD), BF16),
            V((NZ * 16, HD), F32), V((NZ * 16, HD), BF16), V((NZ * 16, HD), BF16),
            V((16, HD), BF16), V((NZ * 16, HD), BF16), V((H + 6, C, HD), BF16),
            V((H, T), jnp.int32), V((H, C), jnp.int32),
            D((4, CH)), D((4, CH, NX - 1)), D((4, CH, NX - 1)), D((4, CH)), D((4, CH)),
            D((4, CH)), D((4, CH)), D((2,)), D((2,)), D((groups, NY + NZ - 1)), D((groups, NY + NZ - 1)),
            D((5, NY)), D((5, NY)), D((2,)),
        ]
        wide = jax.ShapeDtypeStruct((T, WD), BF16)
        hbm = pl.BlockSpec(memory_space=pltpu.HBM)
        vmem = pl.BlockSpec(memory_space=pltpu.VMEM)
        ins = (q, k, v, g, clusters, owner_slot)
        outs = pl.pallas_call(
            functools.partial(kernel, dims),
            out_shape=(wide, wide, wide, wide, jax.ShapeDtypeStruct((H, HD), BF16)),
            in_specs=[hbm] * 6,
            out_specs=(vmem,) * 5,
            scratch_shapes=scratch,
            compiler_params=pltpu.CompilerParams(
                collective_id=0, has_side_effects=True, vmem_limit_bytes=40 * 1024 * 1024
            ),
        )(*(pltpu.with_memory_space_constraint(a, pltpu.HBM) for a in ins))
        small = jax.ShapeDtypeStruct((H, HD), BF16)
        outs = pl.pallas_call(
            flush,
            out_shape=(wide, wide, wide, wide, small),
            in_specs=[vmem] * 5,
            out_specs=(hbm,) * 5,
            scratch_shapes=[D((5,))],
            compiler_params=pltpu.CompilerParams(vmem_limit_bytes=8 * 1024 * 1024),
        )(*outs)
        return (*outs[:4], outs[4].reshape(H, 1, HD))

    rows = P(("seq", "head"), None)
    return jax.shard_map(
        body,
        mesh=mesh,
        in_specs=(rows, rows, rows, rows, P("head", "seq"), P("head", None)),
        out_specs=(P("seq", "head"),) * 4 + (P("head", "seq", None),),
        check_vma=False,
    )
```

```python
import functools

import jax
import jax.numpy as jnp
from jax import lax
from jax.experimental import pallas as pl
from jax.experimental.pallas import tpu as pltpu
from jax.sharding import PartitionSpec as P

HEAD_DIM = 128
WINDOW = 512
F32 = jnp.float32
BF16 = jnp.bfloat16
NN = (((1,), (0,)), ((), ()))
NT = (((1,), (1,)), ((), ()))
TN = (((0,), (0,)), ((), ()))


def factors(count):
    return {128: (16, 4, 2), 8: (2, 2, 2)}[count]


def mm(a, b, dims):
    return lax.dot_general(a, b, dims, preferred_element_type=F32)


def split(v):
    hi = v.astype(BF16)
    rest = v - hi.astype(F32)
    mid = rest.astype(BF16)
    return hi, mid, (rest - mid.astype(F32)).astype(BF16)


def join(parts):
    return functools.reduce(lambda a, b: a + b, [p.astype(F32) for p in parts])


def pick(table, lane):
    lanes = lax.broadcasted_iota(jnp.int32, table.shape, 1)
    return jnp.sum(jnp.where(lanes == lane, table, 0.0), axis=1, keepdims=True)


def kernel(
    dims, q_in, k_in, v_in, g_in, clus_in, slot_in, attn_out, dq_out, dk_out, dv_out, cent_out,
    qw, gw, kw, vw, dkw, dvw, mem, wout, bias, bias_t, sta, st,
    cnt, cnt_c, cnt_y, cnt_z,
    sums, sums_c, half, half_b, sums_y, zs, zb, zr, own,
    agz, tmp, hy, cg,
    lb, pay, pay_c, pay_h, pay_b, pay_y, zs2, zb2, zr2,
    blk, agz2, co, clus, slot,
    loc_sem, a2a_s, a2a_r, far_s, far_r, near_s, near_r, st_s, st_r, cl_s, cl_r, co_s, co_r, ids_sem,
):
    NX, NZ, NY, NC, H, T, HD, CH = dims
    NS = NZ * NY * NC
    C = NS
    RPD = T // NX
    HC = C // NC
    ZR = NZ
    HPC = H // CH
    CW = HPC * HD
    WD = H * HD
    scale = HEAD_DIM ** (-0.5)
    s = lax.axis_index("seq")
    x = lax.axis_index("head")
    c = lax.rem(s, NC)
    y = lax.rem(lax.div(s, NC), NY)
    z = lax.div(s, NC * NY)

    def at(zz, yy, cc):
        return ((zz * NY + yy) * NC + cc, x)

    def seq_off(k):
        return (lax.rem(s + k + NS, NS), x)

    def rc(src, dst, ss, rs, dev):
        return pltpu.make_async_remote_copy(
            src_ref=src, dst_ref=dst, send_sem=ss, recv_sem=rs, device_id=dev,
            device_id_type=pl.DeviceIdType.MESH,
        )

    ids = (
        pltpu.make_async_copy(clus_in, clus, ids_sem.at[0]),
        pltpu.make_async_copy(slot_in, slot, ids_sem.at[1]),
    )
    for cp in ids:
        cp.start()
    bar = pltpu.get_barrier_semaphore()

    def hello(dev):
        pl.semaphore_signal(bar, inc=1, device_id=dev, device_id_type=pl.DeviceIdType.MESH)

    for d in range(1, NX):
        hello((s, lax.rem(x + d, NX)))
    hello(at(z, y, 1 - c))
    for d in range(1, NY):
        hello(at(z, lax.rem(y + d, NY), c))

    def hello_z(d, carry):
        hello(at(lax.rem(z + d, NZ), y, c))
        return carry

    lax.fori_loop(1, NZ, hello_z, 0)
    for k in (-2, -1, 1, 2):
        hello(seq_off(k))

    pl.semaphore_wait(bar, (NX - 1) + 1 + (NY - 1) + (NZ - 1) + 4)

    plan = ((k_in, kw, 2 * T), (v_in, vw, 2 * T), (q_in, qw, 0), (g_in, gw, 0))

    def a2a_slices(i, ch, to):
        src, dst, first = plan[i]
        return (
            src.at[:, pl.ds(pl.multiple_of(to * WD + ch * CW, CW), CW)],
            dst.at[pl.ds(pl.multiple_of(first + x * RPD, RPD), RPD), pl.ds(ch * CW, CW)],
        )

    def a2a(i, ch, d):
        to = lax.rem(x + d, NX)
        return rc(*a2a_slices(i, ch, to), a2a_s.at[i, ch, d - 1], a2a_r.at[i, ch, d - 1], (s, to))

    def own_copy(i, ch):
        return pltpu.make_async_copy(*a2a_slices(i, ch, x), loc_sem.at[i, ch])

    KV, QG = (0, 1), (2, 3)
    order = [(KV, 0)] + [(QG, ch) for ch in range(CH)] + [(KV, ch) for ch in range(1, CH)]
    for pair, ch in order:
        for i in pair:
            for d in range(1, NX):
                a2a(i, ch, d).start()
            own_copy(i, ch).start()

    def a2a_wait(ch, pair):
        for i in pair:
            for d in range(1, NX):
                a2a(i, ch, d).wait_recv()
            own_copy(i, ch).wait()

    def far(i, ch):
        buf, first = plan[i][1], plan[i][2]
        cols = pl.ds(ch * CW, CW)
        return rc(
            buf.at[pl.ds(first, T), cols], buf.at[pl.ds(2 * T - first, T), cols],
            far_s.at[i, ch], far_r.at[i, ch], seq_off(2 if i < 2 else -2),
        )

    def near(i, ch):
        buf = plan[i][1]
        cols = pl.ds(ch * CW, CW)
        first = 2 * T * (1 - c)
        return rc(
            buf.at[pl.ds(pl.multiple_of(first, T), T), cols], buf.at[pl.ds(T, T), cols],
            near_s.at[i, ch], near_r.at[i, ch], at(z, y, 1 - c),
        )

    def send_near(ch, core, pair):
        @pl.when(c == core)
        def _():
            for i in pair:
                near(i, ch).start()

    def halo_start(ch):
        for i in range(4):
            far(i, ch).start()
        send_near(ch, 0, (0, 1))
        send_near(ch, 1, (2, 3))

    def halo_pass(ch):
        for i in range(4):
            far(i, ch).wait_recv()
        send_near(ch, 1, (0, 1))
        send_near(ch, 0, (2, 3))

    for cp in ids:
        cp.wait()
    row_ids = lax.broadcasted_iota(jnp.int32, (C, C), 0)
    clu_ids = lax.broadcasted_iota(jnp.int32, (C, T), 0)

    def members(h, carry):
        r = slot[pl.ds(h, 1), :]
        ps = lax.rem(r, NC) * (NY * NZ) + lax.rem(lax.div(r, NC), NY) * NZ + lax.div(r, NC * NY)
        slot_pick = jnp.where(ps == row_ids, 1.0, 0.0).astype(BF16)
        clu_pick = jnp.where(clus[pl.ds(h, 1), :] == clu_ids, 1.0, 0.0).astype(BF16)
        m = mm(slot_pick, clu_pick, NN).astype(BF16)
        mem[h] = m
        cnt[0, pl.ds(h, 1), :] = mm(jnp.ones((8, T), BF16), m, NT)[0:1]
        return carry

    lax.fori_loop(0, H, members, 0)
    qi = lax.broadcasted_iota(jnp.int32, (T, 3 * T), 0)
    kj = lax.broadcasted_iota(jnp.int32, (T, 3 * T), 1)
    allowed = (kj <= qi + 2 * T) & (kj > qi + 2 * T - WINDOW_OF(T)) & (kj >= (2 - s) * T)
    bias[...] = jnp.where(allowed, 0.0, -1e30)
    allowed = (qi <= kj) & (qi > kj - WINDOW_OF(T)) & (kj < (NS - s) * T)
    bias_t[...] = jnp.where(allowed, 0.0, -1e30)

    def c_copy(g, src, dst):
        return rc(src, dst, cl_s.at[g, 0], cl_r.at[g, 0], at(z, y, 1 - c))

    def y_copy(g, d, src, dst):
        return rc(src, dst, cl_s.at[g, d], cl_r.at[g, d], at(z, lax.rem(y + d, NY), c))

    def z_copy(g, d, src, dst):
        return rc(
            src, dst, cl_s.at[g, NY + d - 1], cl_r.at[g, NY + d - 1], at(lax.rem(z + d, NZ), y, c)
        )

    def z_loop(f):
        lax.fori_loop(1, NZ, lambda d, carry: (f(d), carry)[1], 0)

    def q_copy(g, d, src, dst):
        return rc(src, dst, co_s.at[g, d], co_r.at[g, d], at(z, y, 1 - c))

    near_first = sorted(range(1, NY), key=lambda d: (min(d, NY - d), d))
    far_first = near_first[::-1]

    cc0 = c_copy(0, cnt.at[0], cnt_c)
    cc0.start()
    cc0.wait()
    cnt[1] = cnt[0] + cnt_c[...]
    for d in range(1, NY):
        y_copy(0, d, cnt.at[1], cnt_y.at[d - 1]).start()
    total = cnt[1]
    for d in range(1, NY):
        y_copy(0, d, cnt.at[1], cnt_y.at[d - 1]).wait_recv()
        total = total + cnt_y[d - 1]
    cnt[2] = total
    z_loop(lambda d: z_copy(0, d, cnt.at[2], cnt_z.at[d - 1]).start())

    def head_cols(h):
        return pl.ds(pl.multiple_of(h * HD, HD), HD)

    own_rows = pl.ds(0, T)

    def add_sums(h, carry):
        m = mem[h]
        sums[h] = mm(m, qw[own_rows, head_cols(h)], NN)
        sums[H + h] = mm(m, gw[own_rows, head_cols(h)], NN)
        return carry

    for ch in range(CH):
        if ch == 0:
            a2a_wait(0, KV)
        a2a_wait(ch, QG)
        if ch == 0:
            halo_start(0)
        lax.fori_loop(ch * HPC, (ch + 1) * HPC, add_sums, 0)
    my_half = pl.ds(pl.multiple_of(c * HC, HC), HC)
    their_half = pl.ds(pl.multiple_of((1 - c) * HC, HC), HC)
    def half_rows(core, yy):
        return pl.ds(pl.multiple_of(core * HC + yy * ZR, ZR), ZR)

    def y_rows(yy):
        return pl.ds(pl.multiple_of(yy * ZR, ZR), ZR)

    def up(d):
        return lax.rem(y + d, NY)

    def down(d):
        return lax.rem(y - d + NY, NY)

    def c1(d):
        return q_copy(0, d, sums.at[:, half_rows(1 - c, up(d)), :], sums_c.at[:, y_rows(up(d)), :])

    def y1(d):
        return y_copy(1, d, half_b.at[:, y_rows(up(d)), :], sums_y.at[d - 1])

    for d in far_first + [0]:
        c1(d).start()
    for d in far_first + [0]:
        c1(d).wait_recv()
        v = sums[:, half_rows(c, up(d)), :] + sums_c[:, y_rows(up(d)), :]
        if d:
            half_b[:, y_rows(up(d)), :] = v.astype(BF16)
            y1(d).start()
        else:
            half[:, y_rows(y), :] = v
    for d in range(1, NY):
        y1(d).wait_recv()
    for p in range(2 * H):
        v = half[p, y_rows(y), :]
        for d in range(1, NY):
            v = v + sums_y[d - 1, p].astype(F32)
        zs[pl.ds(p, NZ, stride=2 * H), :] = v

    def z1(d):
        to = lax.rem(z + d, NZ)
        rows = pl.ds(pl.multiple_of(to * 2 * H, 2 * H), 2 * H)
        return z_copy(1, d, zb.at[rows, :], zr.at[d - 1])

    zb[...] = zs[...].astype(BF16)
    z_loop(lambda d: z1(d).start())
    a2a_wait(1, KV)
    halo_start(1)
    halo_pass(0)

    def near_wait(ch):
        for i in range(4):
            near(i, ch).wait_recv()

    def queries(ch):
        near_wait(ch)
        lax.fori_loop(ch * HPC, (ch + 1) * HPC, query_side, 0)


    own_keys = pl.ds(2 * T, T)
    lanes_t = lax.broadcasted_iota(jnp.int32, (T, HD), 1)

    def query_side(h, carry):
        cols = head_cols(h)
        k, v = kw[:, cols], vw[:, cols]
        t = mm(qw[own_rows, cols], k, NT) * scale + bias[...]
        m = jnp.max(t, axis=1, keepdims=True)
        e = jnp.exp(t - m)
        rl = 1.0 / jnp.sum(e, axis=1, keepdims=True)
        p = e * rl
        wout[:, cols] = mm(p.astype(BF16), v, NN)
        dp = mm(gw[own_rows, cols], v, NT)
        delta = jnp.sum(p * dp, axis=1, keepdims=True)
        ds = (p * (dp - delta) * scale).astype(BF16)
        dq_out[:, cols] = mm(ds, k, NN).astype(BF16)
        old = jnp.where(lanes_t == h, m, sta[...])
        old = jnp.where(lanes_t == H + h, rl, old)
        sta[...] = jnp.where(lanes_t == 2 * H + h, delta, old)
        return carry

    def key_side(n, h, carry):
        cols = head_cols(h)
        q, g = qw[:, cols], gw[:, cols]
        t = mm(kw[own_keys, cols], q, NT) * scale + bias_t[...]
        p = jnp.exp(t - st[n, pl.ds(h, 1), :]) * st[n, pl.ds(H + h, 1), :]
        dp = mm(vw[own_keys, cols], g, NT)
        ds = (p * (dp - st[n, pl.ds(2 * H + h, 1), :]) * scale).astype(BF16)
        dkw[:, cols] = mm(ds, q, NN)
        dvw[:, cols] = mm(p.astype(BF16), g, NN)
        return carry

    def stat(n, o):
        return rc(
            st.at[n, :, pl.ds(0, T)], st.at[n, :, pl.ds(o * T, T)],
            st_s.at[n, o - 1], st_r.at[n, o - 1], seq_off(-o),
        )

    def send_stats(n):
        st[n, :, 0:T] = jnp.transpose(sta[...])[0 : 3 * H]
        for o in (1, 2):
            stat(n, o).start()

    def keys(n, first, last):
        for o in (1, 2):
            stat(n, o).wait_recv()
        lax.fori_loop(first * HPC, last * HPC, functools.partial(key_side, n), 0)

    sta[...] = jnp.zeros((T, HD), F32)
    queries(0)
    z_loop(lambda d: z_copy(0, d, cnt.at[2], cnt_z.at[d - 1]).wait_recv())
    total = lax.fori_loop(0, NZ - 1, lambda d, t: t + cnt_z[d], cnt[2])
    count = pick(total, c * HC + y * ZR + z)

    z_loop(lambda d: z1(d).wait_recv())
    mine = lax.fori_loop(
        0, NZ - 1, lambda d, t: t + zr[d].astype(F32), zs[pl.ds(pl.multiple_of(z * 2 * H, 2 * H), 2 * H), :]
    )
    centroid = mine[0:H] / count
    cent_out[...] = centroid.astype(BF16)
    own[0:H, :] = centroid
    own[H : 2 * H, :] = mine[H:]
    agz[z] = own[...].astype(BF16)

    def z2(d):
        return z_copy(2, d, agz.at[z], agz.at[z])

    z_loop(lambda d: z2(d).start())
    for ch in range(2, CH):
        a2a_wait(ch, KV)
    halo_start(2)
    halo_pass(1)
    queries(1)
    z_loop(lambda d: z2(d).wait_recv())
    for i in range(NZ):
        tmp[i * 2 * H : (i + 1) * 2 * H, :] = agz[i].astype(F32)
    for p in range(2 * H):
        hy[p] = tmp[pl.ds(p, NZ, stride=2 * H), :].astype(BF16)
    quarter = half_rows(c, y)
    sides = (pl.ds(0, H), pl.ds(H, H))

    def y2(side, d):
        return y_copy(2 + 3 * side, d, hy.at[sides[side]], cg.at[sides[side], quarter, :])

    def c2(side, d):
        where = cg.at[sides[side], half_rows(c, down(d)), :]
        return q_copy(1 + side, d, hy.at[sides[side]] if d == 0 else where, where)

    for side in range(2):
        for d in far_first:
            y2(side, d).start()
    c2(0, 0).start()
    cg[:, quarter, :] = hy[...]
    halo_pass(2)
    for d in near_first:
        y2(0, d).wait_recv()
        c2(0, d).start()
    for d in range(NY):
        c2(0, d).wait_recv()

    lanes_c = lax.broadcasted_iota(jnp.int32, (C, HD), 1)
    tops, masses = jnp.zeros((C, HD), F32), jnp.zeros((C, HD), F32)
    for h in range(H):
        lg = mm(cg[h], kw[own_keys, head_cols(h)], NT) * scale
        lb[h] = lg
        m = jnp.max(lg, axis=1, keepdims=True)
        e = jnp.exp(lg - m)
        pay[h] = mm(e.astype(BF16), vw[own_keys, head_cols(h)], NN)
        tops = jnp.where(lanes_c == h, m, tops)
        masses = jnp.where(lanes_c == h, jnp.sum(e, axis=1, keepdims=True), masses)
    pay[H] = tops
    pay[H + 1] = masses
    def c3(d):
        return q_copy(3, d, pay.at[:, half_rows(1 - c, up(d)), :], pay_c.at[:, y_rows(up(d)), :])

    def y3(d):
        return y_copy(3, d, pay_b.at[:, y_rows(up(d)), :], pay_y.at[d - 1])

    for d in far_first + [0]:
        c3(d).start()
    c2(1, 0).start()
    for d in near_first:
        y2(1, d).wait_recv()
        c2(1, d).start()
    for d in far_first + [0]:
        c3(d).wait_recv()
        mine_q, rows = half_rows(c, up(d)), y_rows(up(d))
        ma, mb = pay[H, mine_q, :], pay_c[H, rows, :]
        top = jnp.maximum(ma, mb)
        fa, fb = jnp.exp(ma - top), jnp.exp(mb - top)
        mass = pay[H + 1, mine_q, :] * fa + pay_c[H + 1, rows, :] * fb
        if d:
            for n, v in enumerate(split(top) + split(mass)):
                pay_b[H + n, rows, :] = v
        else:
            pay_h[H, rows, :] = top
            pay_h[H + 1, rows, :] = mass
        for h in range(H):
            v = pay[h, mine_q, :] * fa[:, h : h + 1] + pay_c[h, rows, :] * fb[:, h : h + 1]
            if d:
                pay_b[h, rows, :] = v.astype(BF16)
            else:
                pay_h[h, rows, :] = v
        if d:
            y3(d).start()

    queries(2)
    send_stats(0)
    for d in range(1, NY):
        y3(d).wait_recv()
    ms = [pay_h[H, y_rows(y), :]] + [join([pay_y[d, H + n] for n in range(3)]) for d in range(NY - 1)]
    ls = [pay_h[H + 1, y_rows(y), :]] + [
        join([pay_y[d, H + 3 + n] for n in range(3)]) for d in range(NY - 1)
    ]
    top = functools.reduce(jnp.maximum, ms)
    fs = [jnp.exp(m - top) for m in ms]
    for h in range(H):
        v = pay_h[h, y_rows(y), :] * fs[0][:, h : h + 1]
        for d in range(NY - 1):
            v = v + pay_y[d, h].astype(F32) * fs[d + 1][:, h : h + 1]
        zs2[pl.ds(h, NZ, stride=16), :] = v
    mass = functools.reduce(lambda a, b: a + b, [a * b for a, b in zip(ls, fs)])
    for n, v in enumerate(split(top) + split(mass)):
        zs2[pl.ds(H + n, NZ, stride=16), :] = v.astype(F32)
    for p in range(H + 6, 16):
        zs2[pl.ds(p, NZ, stride=16), :] = jnp.zeros((NZ, HD), F32)
    zb2[...] = zs2[...].astype(BF16)

    def z3(d):
        to = lax.rem(z + d, NZ)
        rows = pl.ds(pl.multiple_of(to * 16, 16), 16)
        return z_copy(3, d, zb2.at[rows, :], zr2.at[pl.ds(pl.multiple_of(d * 16, 16), 16), :])

    z_loop(lambda d: z3(d).start())
    zr2[0:16, :] = zb2[pl.ds(pl.multiple_of(z * 16, 16), 16), :]

    halo_start(3)
    keys(0, 0, 3)
    z_loop(lambda d: z3(d).wait_recv())
    tmp[0 : NZ * 16, :] = zr2[...].astype(F32)
    mz = join([tmp[pl.ds(H + n, NZ, stride=16), :] for n in range(3)])
    lz = join([tmp[pl.ds(H + 3 + n, NZ, stride=16), :] for n in range(3)])
    topz = jnp.max(mz, axis=0, keepdims=True)
    fz = jnp.exp(mz - topz)
    lrow = jnp.sum(lz * fz, axis=0, keepdims=True)
    diag = lax.broadcasted_iota(jnp.int32, (H, HD), 0) == lax.broadcasted_iota(
        jnp.int32, (H, HD), 1
    )

    def column(row):
        return jnp.sum(jnp.where(diag, row, 0.0), axis=1, keepdims=True)

    acc = jnp.zeros((H, HD), F32)
    for i in range(NZ):
        acc = acc + tmp[i * 16 : i * 16 + H, :] * column(fz[i : i + 1, :])
    c_out = acc / column(lrow)
    grad = own[H : 2 * H, :].astype(BF16).astype(F32)
    c_delta = jnp.sum(grad * c_out, axis=1, keepdims=True)
    tmp[0:16, :] = jnp.zeros((16, HD), F32)
    tmp[0:H, :] = c_out
    delta_row = jnp.sum(jnp.where(diag, c_delta, 0.0), axis=0, keepdims=True)
    for n, v in enumerate(split(topz + jnp.log(jnp.where(lrow > 0.0, lrow, 1.0))) + split(delta_row)):
        tmp[H + n : H + n + 1, :] = v.astype(F32)
    blk[...] = tmp[0:16, :].astype(BF16)

    my_rows16 = pl.ds(pl.multiple_of(z * 16, 16), 16)

    def z4(d):
        return z_copy(4, d, blk, agz2.at[my_rows16, :])

    z_loop(lambda d: z4(d).start())
    agz2[my_rows16, :] = blk[...]
    halo_pass(3)
    queries(3)
    send_stats(1)
    for ch in range(CH):
        for i in range(4):
            for d in range(1, NX):
                a2a(i, ch, d).wait_send()
            far(i, ch).wait_send()
            near(i, ch).wait_send()
    for d in range(1, NY):
        y_copy(0, d, cnt.at[1], cnt_y.at[d - 1]).wait_send()
        for cp in (y1(d), y2(0, d), y2(1, d), y3(d)):
            cp.wait_send()
    for d in range(NY):
        for cp in (c1(d), c2(0, d), c2(1, d), c3(d)):
            cp.wait_send()

    def drain(d):
        z_copy(0, d, cnt.at[2], cnt_z.at[d - 1]).wait_send()
        z1(d).wait_send()
        z2(d).wait_send()
        z3(d).wait_send()

    z_loop(drain)
    z_loop(lambda d: z4(d).wait())
    tmp[0 : NZ * 16, :] = agz2[...].astype(F32)
    for p in range(H + 6):
        co[p, quarter, :] = tmp[pl.ds(p, NZ, stride=16), :].astype(BF16)

    def y4(d):
        return y_copy(4, d, co.at[:, quarter, :], co.at[:, quarter, :])

    def c4(d):
        where = co.at[:, half_rows(c, down(d)), :]
        return q_copy(4, d, where, where)

    for d in far_first:
        y4(d).start()
    c4(0).start()
    keys(1, 3, CH)
    for d in near_first:
        y4(d).wait_recv()
        c4(d).start()
    for d in range(NY):
        c2(1, d).wait_recv()
    for d in range(NY):
        c4(d).wait_recv()

    lse = join([co[H + n] for n in range(3)])
    deltas = join([co[H + 3 + n] for n in range(3)])
    for h in range(H):
        cols = head_cols(h)
        w = jnp.exp(lb[h] - pick(lse, h))
        dw = mm(cg[H + h], vw[own_keys, cols], NT)
        dl = (w * (dw - pick(deltas, h)) * scale).astype(BF16)
        attn_out[:, cols] = (wout[:, cols] + mm(mem[h], co[h], TN)).astype(BF16)
        dk_out[:, cols] = (dkw[:, cols] + mm(dl, cg[h], TN)).astype(BF16)
        dv_out[:, cols] = (dvw[:, cols] + mm(w.astype(BF16), cg[H + h], TN)).astype(BF16)

    for d in range(1, NY):
        y4(d).wait_send()
    for d in range(NY):
        c4(d).wait_send()
    for n in range(2):
        for o in (1, 2):
            stat(n, o).wait_send()


def flush(*refs):
    sem = refs[10]
    copies = [pltpu.make_async_copy(refs[i], refs[5 + i], sem.at[i]) for i in range(5)]
    for cp in copies:
        cp.start()
    for cp in copies:
        cp.wait()


def WINDOW_OF(tokens):
    return WINDOW if tokens == 256 else 2 * tokens


def solution(mesh):
    NX = mesh.shape["head"]
    NZ, NY, NC = factors(mesh.shape["seq"])
    HD, CH = HEAD_DIM, 4

    def body(q, k, v, g, clusters, owner_slot):
        H, T = clusters.shape
        C = owner_slot.shape[1]
        WD = H * HD
        HC, ZR = C // NC, NZ
        dims = (NX, NZ, NY, NC, H, T, HD, CH)
        V, D = pltpu.VMEM, pltpu.SemaphoreType.DMA
        groups = 6
        scratch = [
            V((3 * T, WD), BF16), V((3 * T, WD), BF16), V((3 * T, WD), BF16), V((3 * T, WD), BF16),
            V((T, WD), F32), V((T, WD), F32), V((H, C, T), BF16),
            V((T, WD), F32), V((T, 3 * T), F32), V((T, 3 * T), F32), V((T, HD), F32),
            V((2, 3 * H, 3 * T), F32),
            V((3, H, C), F32), V((H, C), F32), V((NY - 1, H, C), F32), V((NZ - 1, H, C), F32),
            V((2 * H, C, HD), F32), V((2 * H, HC, HD), F32), V((2 * H, HC, HD), F32),
            V((2 * H, HC, HD), BF16), V((NY - 1, 2 * H, ZR, HD), BF16), V((NZ * 2 * H, HD), F32),
            V((NZ * 2 * H, HD), BF16), V((NZ - 1, 2 * H, HD), BF16), V((2 * H, HD), F32),
            V((NZ, 2 * H, HD), BF16), V((NZ * 16, HD), F32), V((2 * H, NZ, HD), BF16),
            V((2 * H, C, HD), BF16),
            V((H, C, T), F32), V((H + 2, C, HD), F32), V((H + 2, HC, HD), F32),
            V((H + 2, HC, HD), F32), V((H + 6, HC, HD), BF16), V((NY - 1, H + 6, ZR, HD), BF16),
            V((NZ * 16, HD), F32), V((NZ * 16, HD), BF16), V((NZ * 16, HD), BF16),
            V((16, HD), BF16), V((NZ * 16, HD), BF16), V((H + 6, C, HD), BF16),
            V((H, T), jnp.int32), V((H, C), jnp.int32),
            D((4, CH)), D((4, CH, NX - 1)), D((4, CH, NX - 1)), D((4, CH)), D((4, CH)),
            D((4, CH)), D((4, CH)), D((2, 2)), D((2, 2)), D((groups, NY + NZ - 1)), D((groups, NY + NZ - 1)),
            D((5, NY)), D((5, NY)), D((2,)),
        ]
        wide = jax.ShapeDtypeStruct((T, WD), BF16)
        hbm = pl.BlockSpec(memory_space=pltpu.HBM)
        vmem = pl.BlockSpec(memory_space=pltpu.VMEM)
        ins = (q, k, v, g, clusters, owner_slot)
        outs = pl.pallas_call(
            functools.partial(kernel, dims),
            out_shape=(wide, wide, wide, wide, jax.ShapeDtypeStruct((H, HD), BF16)),
            in_specs=[hbm] * 6,
            out_specs=(vmem,) * 5,
            scratch_shapes=scratch,
            compiler_params=pltpu.CompilerParams(
                collective_id=0, has_side_effects=True, vmem_limit_bytes=40 * 1024 * 1024
            ),
        )(*(pltpu.with_memory_space_constraint(a, pltpu.HBM) for a in ins))
        small = jax.ShapeDtypeStruct((H, HD), BF16)
        outs = pl.pallas_call(
            flush,
            out_shape=(wide, wide, wide, wide, small),
            in_specs=[vmem] * 5,
            out_specs=(hbm,) * 5,
            scratch_shapes=[D((5,))],
            compiler_params=pltpu.CompilerParams(vmem_limit_bytes=8 * 1024 * 1024),
        )(*outs)
        return (*outs[:4], outs[4].reshape(H, 1, HD))

    rows = P(("seq", "head"), None)
    return jax.shard_map(
        body,
        mesh=mesh,
        in_specs=(rows, rows, rows, rows, P("head", "seq"), P("head", None)),
        out_specs=(P("seq", "head"),) * 4 + (P("head", "seq", None),),
        check_vma=False,
    )
```

```python
import functools

import jax
import jax.numpy as jnp
from jax import lax
from jax.experimental import pallas as pl
from jax.experimental.pallas import tpu as pltpu
from jax.sharding import PartitionSpec as P

HEAD_DIM = 128
WINDOW = 512
F32 = jnp.float32
BF16 = jnp.bfloat16
NN = (((1,), (0,)), ((), ()))
NT = (((1,), (1,)), ((), ()))
TN = (((0,), (0,)), ((), ()))


def factors(count):
    return {128: (16, 4, 2), 8: (2, 2, 2)}[count]


def mm(a, b, dims):
    return lax.dot_general(a, b, dims, preferred_element_type=F32)


def split(v):
    hi = v.astype(BF16)
    rest = v - hi.astype(F32)
    mid = rest.astype(BF16)
    return hi, mid, (rest - mid.astype(F32)).astype(BF16)


def join(parts):
    return functools.reduce(lambda a, b: a + b, [p.astype(F32) for p in parts])


def pick(table, lane):
    lanes = lax.broadcasted_iota(jnp.int32, table.shape, 1)
    return jnp.sum(jnp.where(lanes == lane, table, 0.0), axis=1, keepdims=True)


def kernel(
    dims, q_in, k_in, v_in, g_in, clus_in, slot_in, attn_out, dq_out, dk_out, dv_out, cent_out,
    qw, gw, kw, vw, dkw, dvw, mem, wout, bias, bias_t, sta, st,
    cnt, cnt_c, cnt_y, cnt_z,
    sums, sums_b, sums_c, half, half_b, sums_y, zs, zb, zr, own,
    agz, tmp, hy, cg,
    lb, dws, pay, pay_c, pay_h, pay_b, pay_y, zs2, zb2, zr2,
    blk, agz2, co, clus, slot,
    loc_sem, a2a_s, a2a_r, far_s, far_r, near_s, near_r, st_s, st_r, cl_s, cl_r, co_s, co_r, ids_sem,
):
    NX, NZ, NY, NC, H, T, HD, CH = dims
    NS = NZ * NY * NC
    C = NS
    RPD = T // NX
    HC = C // NC
    ZR = NZ
    HPC = H // CH
    CW = HPC * HD
    WD = H * HD
    scale = HEAD_DIM ** (-0.5)
    s = lax.axis_index("seq")
    x = lax.axis_index("head")
    c = lax.rem(s, NC)
    y = lax.rem(lax.div(s, NC), NY)
    z = lax.div(s, NC * NY)

    def at(zz, yy, cc):
        return ((zz * NY + yy) * NC + cc, x)

    def seq_off(k):
        return (lax.rem(s + k + NS, NS), x)

    def rc(src, dst, ss, rs, dev):
        return pltpu.make_async_remote_copy(
            src_ref=src, dst_ref=dst, send_sem=ss, recv_sem=rs, device_id=dev,
            device_id_type=pl.DeviceIdType.MESH,
        )

    ids = (
        pltpu.make_async_copy(clus_in, clus, ids_sem.at[0]),
        pltpu.make_async_copy(slot_in, slot, ids_sem.at[1]),
    )
    for cp in ids:
        cp.start()
    bar = pltpu.get_barrier_semaphore()

    def hello(dev):
        pl.semaphore_signal(bar, inc=1, device_id=dev, device_id_type=pl.DeviceIdType.MESH)

    for d in range(1, NX):
        hello((s, lax.rem(x + d, NX)))
    hello(at(z, y, 1 - c))
    for d in range(1, NY):
        hello(at(z, lax.rem(y + d, NY), c))

    def hello_z(d, carry):
        hello(at(lax.rem(z + d, NZ), y, c))
        return carry

    lax.fori_loop(1, NZ, hello_z, 0)
    for k in (-2, -1, 1, 2):
        hello(seq_off(k))

    pl.semaphore_wait(bar, (NX - 1) + 1 + (NY - 1) + (NZ - 1) + 4)

    plan = ((k_in, kw, 2 * T), (v_in, vw, 2 * T), (q_in, qw, 0), (g_in, gw, 0))

    def a2a_slices(i, ch, to):
        src, dst, first = plan[i]
        return (
            src.at[:, pl.ds(pl.multiple_of(to * WD + ch * CW, CW), CW)],
            dst.at[pl.ds(pl.multiple_of(first + x * RPD, RPD), RPD), pl.ds(ch * CW, CW)],
        )

    def a2a(i, ch, d):
        to = lax.rem(x + d, NX)
        return rc(*a2a_slices(i, ch, to), a2a_s.at[i, ch, d - 1], a2a_r.at[i, ch, d - 1], (s, to))

    def own_copy(i, ch):
        return pltpu.make_async_copy(*a2a_slices(i, ch, x), loc_sem.at[i, ch])

    KV, QG = (0, 1), (2, 3)
    order = [(KV, 0)] + [(QG, ch) for ch in range(CH)] + [(KV, ch) for ch in range(1, CH)]
    for pair, ch in order:
        for i in pair:
            for d in range(1, NX):
                a2a(i, ch, d).start()
            own_copy(i, ch).start()

    def a2a_wait(ch, pair):
        for i in pair:
            for d in range(1, NX):
                a2a(i, ch, d).wait_recv()
            own_copy(i, ch).wait()

    def far(i, ch):
        buf, first = plan[i][1], plan[i][2]
        cols = pl.ds(ch * CW, CW)
        return rc(
            buf.at[pl.ds(first, T), cols], buf.at[pl.ds(2 * T - first, T), cols],
            far_s.at[i, ch], far_r.at[i, ch], seq_off(2 if i < 2 else -2),
        )

    def near(i, ch):
        buf = plan[i][1]
        cols = pl.ds(ch * CW, CW)
        first = 2 * T * (1 - c)
        return rc(
            buf.at[pl.ds(pl.multiple_of(first, T), T), cols], buf.at[pl.ds(T, T), cols],
            near_s.at[i, ch], near_r.at[i, ch], at(z, y, 1 - c),
        )

    def send_near(ch, core, pair):
        @pl.when(c == core)
        def _():
            for i in pair:
                near(i, ch).start()

    def halo_start(ch):
        for i in range(4):
            far(i, ch).start()
        send_near(ch, 0, (0, 1))
        send_near(ch, 1, (2, 3))

    def halo_pass(ch):
        for i in range(4):
            far(i, ch).wait_recv()
        send_near(ch, 1, (0, 1))
        send_near(ch, 0, (2, 3))

    for cp in ids:
        cp.wait()
    row_ids = lax.broadcasted_iota(jnp.int32, (C, C), 0)
    clu_ids = lax.broadcasted_iota(jnp.int32, (C, T), 0)

    def members(h, carry):
        r = slot[pl.ds(h, 1), :]
        ps = lax.rem(r, NC) * (NY * NZ) + lax.rem(lax.div(r, NC), NY) * NZ + lax.div(r, NC * NY)
        slot_pick = jnp.where(ps == row_ids, 1.0, 0.0).astype(BF16)
        clu_pick = jnp.where(clus[pl.ds(h, 1), :] == clu_ids, 1.0, 0.0).astype(BF16)
        m = mm(slot_pick, clu_pick, NN).astype(BF16)
        mem[h] = m
        cnt[0, pl.ds(h, 1), :] = mm(jnp.ones((8, T), BF16), m, NT)[0:1]
        return carry

    lax.fori_loop(0, H, members, 0)
    qi = lax.broadcasted_iota(jnp.int32, (T, 3 * T), 0)
    kj = lax.broadcasted_iota(jnp.int32, (T, 3 * T), 1)
    allowed = (kj <= qi + 2 * T) & (kj > qi + 2 * T - WINDOW_OF(T)) & (kj >= (2 - s) * T)
    bias[...] = jnp.where(allowed, 0.0, -1e30)
    allowed = (qi <= kj) & (qi > kj - WINDOW_OF(T)) & (kj < (NS - s) * T)
    bias_t[...] = jnp.where(allowed, 0.0, -1e30)

    def c_copy(g, src, dst):
        return rc(src, dst, cl_s.at[g, 0], cl_r.at[g, 0], at(z, y, 1 - c))

    def y_copy(g, d, src, dst):
        return rc(src, dst, cl_s.at[g, d], cl_r.at[g, d], at(z, lax.rem(y + d, NY), c))

    def z_copy(g, d, src, dst):
        return rc(
            src, dst, cl_s.at[g, NY + d - 1], cl_r.at[g, NY + d - 1], at(lax.rem(z + d, NZ), y, c)
        )

    def z_loop(f):
        lax.fori_loop(1, NZ, lambda d, carry: (f(d), carry)[1], 0)

    def q_copy(g, d, src, dst):
        return rc(src, dst, co_s.at[g, d], co_r.at[g, d], at(z, y, 1 - c))

    near_first = sorted(range(1, NY), key=lambda d: (min(d, NY - d), d))
    far_first = near_first[::-1]

    cc0 = c_copy(0, cnt.at[0], cnt_c)
    cc0.start()
    cc0.wait()
    cnt[1] = cnt[0] + cnt_c[...]
    for d in range(1, NY):
        y_copy(0, d, cnt.at[1], cnt_y.at[d - 1]).start()
    total = cnt[1]
    for d in range(1, NY):
        y_copy(0, d, cnt.at[1], cnt_y.at[d - 1]).wait_recv()
        total = total + cnt_y[d - 1]
    cnt[2] = total
    z_loop(lambda d: z_copy(0, d, cnt.at[2], cnt_z.at[d - 1]).start())

    def head_cols(h):
        return pl.ds(pl.multiple_of(h * HD, HD), HD)

    own_rows = pl.ds(0, T)

    def add_sums(h, carry):
        m = mem[h]
        for row, buf in ((h, qw), (H + h, gw)):
            total = mm(m, buf[own_rows, head_cols(h)], NN)
            sums[row] = total
            sums_b[row] = total.astype(BF16)
        return carry

    for ch in range(CH):
        if ch == 0:
            a2a_wait(0, KV)
        a2a_wait(ch, QG)
        if ch == 0:
            halo_start(0)
        lax.fori_loop(ch * HPC, (ch + 1) * HPC, add_sums, 0)
    my_half = pl.ds(pl.multiple_of(c * HC, HC), HC)
    their_half = pl.ds(pl.multiple_of((1 - c) * HC, HC), HC)
    def half_rows(core, yy):
        return pl.ds(pl.multiple_of(core * HC + yy * ZR, ZR), ZR)

    def y_rows(yy):
        return pl.ds(pl.multiple_of(yy * ZR, ZR), ZR)

    def up(d):
        return lax.rem(y + d, NY)

    def down(d):
        return lax.rem(y - d + NY, NY)

    def c1(d):
        return q_copy(0, d, sums_b.at[:, half_rows(1 - c, up(d)), :], sums_c.at[:, y_rows(up(d)), :])

    def y1(d):
        return y_copy(1, d, half_b.at[:, y_rows(up(d)), :], sums_y.at[d - 1])

    for d in far_first + [0]:
        c1(d).start()
    for d in far_first + [0]:
        c1(d).wait_recv()
        v = sums[:, half_rows(c, up(d)), :] + sums_c[:, y_rows(up(d)), :].astype(F32)
        if d:
            half_b[:, y_rows(up(d)), :] = v.astype(BF16)
            y1(d).start()
        else:
            half[:, y_rows(y), :] = v
    for d in range(1, NY):
        y1(d).wait_recv()
    for p in range(2 * H):
        v = half[p, y_rows(y), :]
        for d in range(1, NY):
            v = v + sums_y[d - 1, p].astype(F32)
        zs[pl.ds(p, NZ, stride=2 * H), :] = v

    def z1(d):
        to = lax.rem(z + d, NZ)
        rows = pl.ds(pl.multiple_of(to * 2 * H, 2 * H), 2 * H)
        return z_copy(1, d, zb.at[rows, :], zr.at[d - 1])

    zb[...] = zs[...].astype(BF16)
    z_loop(lambda d: z1(d).start())
    a2a_wait(1, KV)
    halo_start(1)
    halo_pass(0)

    def near_wait(ch):
        for i in range(4):
            near(i, ch).wait_recv()

    def queries(ch):
        near_wait(ch)
        lax.fori_loop(ch * HPC, (ch + 1) * HPC, query_side, 0)


    own_keys = pl.ds(2 * T, T)
    lanes_t = lax.broadcasted_iota(jnp.int32, (T, HD), 1)

    def query_side(h, carry):
        cols = head_cols(h)
        k, v = kw[:, cols], vw[:, cols]
        t = mm(qw[own_rows, cols], k, NT) * scale + bias[...]
        m = jnp.max(t, axis=1, keepdims=True)
        e = jnp.exp(t - m)
        rl = 1.0 / jnp.sum(e, axis=1, keepdims=True)
        p = e * rl
        wout[:, cols] = mm(p.astype(BF16), v, NN)
        dp = mm(gw[own_rows, cols], v, NT)
        delta = jnp.sum(p * dp, axis=1, keepdims=True)
        ds = (p * (dp - delta) * scale).astype(BF16)
        dq_out[:, cols] = mm(ds, k, NN).astype(BF16)
        old = jnp.where(lanes_t == h, m, sta[...])
        old = jnp.where(lanes_t == H + h, rl, old)
        sta[...] = jnp.where(lanes_t == 2 * H + h, delta, old)
        return carry

    def key_side(n, h, carry):
        cols = head_cols(h)
        q, g = qw[:, cols], gw[:, cols]
        t = mm(kw[own_keys, cols], q, NT) * scale + bias_t[...]
        p = jnp.exp(t - st[n, pl.ds(h, 1), :]) * st[n, pl.ds(H + h, 1), :]
        dp = mm(vw[own_keys, cols], g, NT)
        ds = (p * (dp - st[n, pl.ds(2 * H + h, 1), :]) * scale).astype(BF16)
        dkw[:, cols] = mm(ds, q, NN)
        dvw[:, cols] = mm(p.astype(BF16), g, NN)
        return carry

    def stat(n, o):
        return rc(
            st.at[n, :, pl.ds(0, T)], st.at[n, :, pl.ds(o * T, T)],
            st_s.at[n, o - 1], st_r.at[n, o - 1], seq_off(-o),
        )

    def send_stats(n):
        st[n, :, 0:T] = jnp.transpose(sta[...])[0 : 3 * H]
        for o in (1, 2):
            stat(n, o).start()

    def keys(n, first, last):
        for o in (1, 2):
            stat(n, o).wait_recv()
        lax.fori_loop(first * HPC, last * HPC, functools.partial(key_side, n), 0)

    sta[...] = jnp.zeros((T, HD), F32)
    queries(0)
    z_loop(lambda d: z_copy(0, d, cnt.at[2], cnt_z.at[d - 1]).wait_recv())
    total = lax.fori_loop(0, NZ - 1, lambda d, t: t + cnt_z[d], cnt[2])
    count = pick(total, c * HC + y * ZR + z)

    z_loop(lambda d: z1(d).wait_recv())
    mine = lax.fori_loop(
        0, NZ - 1, lambda d, t: t + zr[d].astype(F32), zs[pl.ds(pl.multiple_of(z * 2 * H, 2 * H), 2 * H), :]
    )
    centroid = mine[0:H] / count
    cent_out[...] = centroid.astype(BF16)
    own[0:H, :] = centroid
    own[H : 2 * H, :] = mine[H:]
    agz[z] = own[...].astype(BF16)

    def z2(d):
        return z_copy(2, d, agz.at[z], agz.at[z])

    z_loop(lambda d: z2(d).start())
    for ch in range(2, CH):
        a2a_wait(ch, KV)
    halo_start(2)
    halo_pass(1)
    queries(1)
    z_loop(lambda d: z2(d).wait_recv())
    for i in range(NZ):
        tmp[i * 2 * H : (i + 1) * 2 * H, :] = agz[i].astype(F32)
    for p in range(2 * H):
        hy[p] = tmp[pl.ds(p, NZ, stride=2 * H), :].astype(BF16)
    quarter = half_rows(c, y)
    sides = (pl.ds(0, H), pl.ds(H, H))

    def y2(side, d):
        return y_copy(2 + 3 * side, d, hy.at[sides[side]], cg.at[sides[side], quarter, :])

    def c2(side, d):
        where = cg.at[sides[side], half_rows(c, down(d)), :]
        return q_copy(1 + side, d, hy.at[sides[side]] if d == 0 else where, where)

    for side in range(2):
        for d in far_first:
            y2(side, d).start()
    c2(0, 0).start()
    cg[:, quarter, :] = hy[...]
    for d in near_first:
        y2(0, d).wait_recv()
        c2(0, d).start()
    for d in range(NY):
        c2(0, d).wait_recv()

    lanes_c = lax.broadcasted_iota(jnp.int32, (C, HD), 1)
    tops, masses = jnp.zeros((C, HD), F32), jnp.zeros((C, HD), F32)
    for h in range(H):
        lg = mm(cg[h], kw[own_keys, head_cols(h)], NT) * scale
        lb[h] = lg
        m = jnp.max(lg, axis=1, keepdims=True)
        e = jnp.exp(lg - m)
        pay[h] = mm(e.astype(BF16), vw[own_keys, head_cols(h)], NN)
        tops = jnp.where(lanes_c == h, m, tops)
        masses = jnp.where(lanes_c == h, jnp.sum(e, axis=1, keepdims=True), masses)
    pay[H] = tops
    pay[H + 1] = masses
    def c3(d):
        return q_copy(3, d, pay.at[:, half_rows(1 - c, up(d)), :], pay_c.at[:, y_rows(up(d)), :])

    def y3(d):
        return y_copy(3, d, pay_b.at[:, y_rows(up(d)), :], pay_y.at[d - 1])

    for d in far_first + [0]:
        c3(d).start()
    c2(1, 0).start()
    for d in near_first:
        y2(1, d).wait_recv()
        c2(1, d).start()
    halo_pass(2)
    for d in far_first + [0]:
        c3(d).wait_recv()
        mine_q, rows = half_rows(c, up(d)), y_rows(up(d))
        ma, mb = pay[H, mine_q, :], pay_c[H, rows, :]
        top = jnp.maximum(ma, mb)
        fa, fb = jnp.exp(ma - top), jnp.exp(mb - top)
        mass = pay[H + 1, mine_q, :] * fa + pay_c[H + 1, rows, :] * fb
        if d:
            for n, v in enumerate(split(top) + split(mass)):
                pay_b[H + n, rows, :] = v
        else:
            pay_h[H, rows, :] = top
            pay_h[H + 1, rows, :] = mass
        for h in range(H):
            v = pay[h, mine_q, :] * fa[:, h : h + 1] + pay_c[h, rows, :] * fb[:, h : h + 1]
            if d:
                pay_b[h, rows, :] = v.astype(BF16)
            else:
                pay_h[h, rows, :] = v
        if d:
            y3(d).start()

    queries(2)
    send_stats(0)
    for d in range(1, NY):
        y3(d).wait_recv()
    ms = [pay_h[H, y_rows(y), :]] + [join([pay_y[d, H + n] for n in range(3)]) for d in range(NY - 1)]
    ls = [pay_h[H + 1, y_rows(y), :]] + [
        join([pay_y[d, H + 3 + n] for n in range(3)]) for d in range(NY - 1)
    ]
    top = functools.reduce(jnp.maximum, ms)
    fs = [jnp.exp(m - top) for m in ms]
    for h in range(H):
        v = pay_h[h, y_rows(y), :] * fs[0][:, h : h + 1]
        for d in range(NY - 1):
            v = v + pay_y[d, h].astype(F32) * fs[d + 1][:, h : h + 1]
        zs2[pl.ds(h, NZ, stride=16), :] = v
    mass = functools.reduce(lambda a, b: a + b, [a * b for a, b in zip(ls, fs)])
    for n, v in enumerate(split(top) + split(mass)):
        zs2[pl.ds(H + n, NZ, stride=16), :] = v.astype(F32)
    for p in range(H + 6, 16):
        zs2[pl.ds(p, NZ, stride=16), :] = jnp.zeros((NZ, HD), F32)
    zb2[...] = zs2[...].astype(BF16)

    def z3(d):
        to = lax.rem(z + d, NZ)
        rows = pl.ds(pl.multiple_of(to * 16, 16), 16)
        return z_copy(3, d, zb2.at[rows, :], zr2.at[pl.ds(pl.multiple_of(d * 16, 16), 16), :])

    z_loop(lambda d: z3(d).start())
    zr2[0:16, :] = zb2[pl.ds(pl.multiple_of(z * 16, 16), 16), :]

    halo_start(3)
    keys(0, 0, 3)
    for d in range(NY):
        c2(1, d).wait_recv()
    for h in range(H):
        dws[h] = mm(cg[H + h], vw[own_keys, head_cols(h)], NT)
    z_loop(lambda d: z3(d).wait_recv())
    tmp[0 : NZ * 16, :] = zr2[...].astype(F32)
    mz = join([tmp[pl.ds(H + n, NZ, stride=16), :] for n in range(3)])
    lz = join([tmp[pl.ds(H + 3 + n, NZ, stride=16), :] for n in range(3)])
    topz = jnp.max(mz, axis=0, keepdims=True)
    fz = jnp.exp(mz - topz)
    lrow = jnp.sum(lz * fz, axis=0, keepdims=True)
    diag = lax.broadcasted_iota(jnp.int32, (H, HD), 0) == lax.broadcasted_iota(
        jnp.int32, (H, HD), 1
    )

    def column(row):
        return jnp.sum(jnp.where(diag, row, 0.0), axis=1, keepdims=True)

    acc = jnp.zeros((H, HD), F32)
    for i in range(NZ):
        acc = acc + tmp[i * 16 : i * 16 + H, :] * column(fz[i : i + 1, :])
    c_out = acc / column(lrow)
    grad = own[H : 2 * H, :].astype(BF16).astype(F32)
    c_delta = jnp.sum(grad * c_out, axis=1, keepdims=True)
    tmp[0:16, :] = jnp.zeros((16, HD), F32)
    tmp[0:H, :] = c_out
    delta_row = jnp.sum(jnp.where(diag, c_delta, 0.0), axis=0, keepdims=True)
    for n, v in enumerate(split(topz + jnp.log(jnp.where(lrow > 0.0, lrow, 1.0))) + split(delta_row)):
        tmp[H + n : H + n + 1, :] = v.astype(F32)
    blk[...] = tmp[0:16, :].astype(BF16)

    my_rows16 = pl.ds(pl.multiple_of(z * 16, 16), 16)

    def z4(d):
        return z_copy(4, d, blk, agz2.at[my_rows16, :])

    z_loop(lambda d: z4(d).start())
    agz2[my_rows16, :] = blk[...]
    halo_pass(3)
    queries(3)
    send_stats(1)
    for ch in range(CH):
        for i in range(4):
            for d in range(1, NX):
                a2a(i, ch, d).wait_send()
            far(i, ch).wait_send()
            near(i, ch).wait_send()
    for d in range(1, NY):
        y_copy(0, d, cnt.at[1], cnt_y.at[d - 1]).wait_send()
        for cp in (y1(d), y2(0, d), y2(1, d), y3(d)):
            cp.wait_send()
    for d in range(NY):
        for cp in (c1(d), c2(0, d), c2(1, d), c3(d)):
            cp.wait_send()

    def drain(d):
        z_copy(0, d, cnt.at[2], cnt_z.at[d - 1]).wait_send()
        z1(d).wait_send()
        z2(d).wait_send()
        z3(d).wait_send()

    z_loop(drain)
    z_loop(lambda d: z4(d).wait())
    tmp[0 : NZ * 16, :] = agz2[...].astype(F32)
    for p in range(H + 6):
        co[p, quarter, :] = tmp[pl.ds(p, NZ, stride=16), :].astype(BF16)

    def y4(d):
        return y_copy(4, d, co.at[:, quarter, :], co.at[:, quarter, :])

    def c4(d):
        where = co.at[:, half_rows(c, down(d)), :]
        return q_copy(4, d, where, where)

    for d in far_first:
        y4(d).start()
    c4(0).start()
    keys(1, 3, CH)
    for d in near_first:
        y4(d).wait_recv()
        c4(d).start()
    for d in range(NY):
        c4(d).wait_recv()

    lse = join([co[H + n] for n in range(3)])
    deltas = join([co[H + 3 + n] for n in range(3)])
    for h in range(H):
        cols = head_cols(h)
        w = jnp.exp(lb[h] - pick(lse, h))
        dl = (w * (dws[h] - pick(deltas, h)) * scale).astype(BF16)
        attn_out[:, cols] = (wout[:, cols] + mm(mem[h], co[h], TN)).astype(BF16)
        dk_out[:, cols] = (dkw[:, cols] + mm(dl, cg[h], TN)).astype(BF16)
        dv_out[:, cols] = (dvw[:, cols] + mm(w.astype(BF16), cg[H + h], TN)).astype(BF16)

    for d in range(1, NY):
        y4(d).wait_send()
    for d in range(NY):
        c4(d).wait_send()
    for n in range(2):
        for o in (1, 2):
            stat(n, o).wait_send()


def flush(*refs):
    sem = refs[10]
    copies = [pltpu.make_async_copy(refs[i], refs[5 + i], sem.at[i]) for i in range(5)]
    for cp in copies:
        cp.start()
    for cp in copies:
        cp.wait()


def WINDOW_OF(tokens):
    return WINDOW if tokens == 256 else 2 * tokens


def solution(mesh):
    NX = mesh.shape["head"]
    NZ, NY, NC = factors(mesh.shape["seq"])
    HD, CH = HEAD_DIM, 4

    def body(q, k, v, g, clusters, owner_slot):
        H, T = clusters.shape
        C = owner_slot.shape[1]
        WD = H * HD
        HC, ZR = C // NC, NZ
        dims = (NX, NZ, NY, NC, H, T, HD, CH)
        V, D = pltpu.VMEM, pltpu.SemaphoreType.DMA
        groups = 6
        scratch = [
            V((3 * T, WD), BF16), V((3 * T, WD), BF16), V((3 * T, WD), BF16), V((3 * T, WD), BF16),
            V((T, WD), F32), V((T, WD), F32), V((H, C, T), BF16),
            V((T, WD), F32), V((T, 3 * T), F32), V((T, 3 * T), F32), V((T, HD), F32),
            V((2, 3 * H, 3 * T), F32),
            V((3, H, C), F32), V((H, C), F32), V((NY - 1, H, C), F32), V((NZ - 1, H, C), F32),
            V((2 * H, C, HD), F32), V((2 * H, C, HD), BF16), V((2 * H, HC, HD), BF16),
            V((2 * H, HC, HD), F32),
            V((2 * H, HC, HD), BF16), V((NY - 1, 2 * H, ZR, HD), BF16), V((NZ * 2 * H, HD), F32),
            V((NZ * 2 * H, HD), BF16), V((NZ - 1, 2 * H, HD), BF16), V((2 * H, HD), F32),
            V((NZ, 2 * H, HD), BF16), V((NZ * 16, HD), F32), V((2 * H, NZ, HD), BF16),
            V((2 * H, C, HD), BF16),
            V((H, C, T), F32), V((H, C, T), F32), V((H + 2, C, HD), F32), V((H + 2, HC, HD), F32),
            V((H + 2, HC, HD), F32), V((H + 6, HC, HD), BF16), V((NY - 1, H + 6, ZR, HD), BF16),
            V((NZ * 16, HD), F32), V((NZ * 16, HD), BF16), V((NZ * 16, HD), BF16),
            V((16, HD), BF16), V((NZ * 16, HD), BF16), V((H + 6, C, HD), BF16),
            V((H, T), jnp.int32), V((H, C), jnp.int32),
            D((4, CH)), D((4, CH, NX - 1)), D((4, CH, NX - 1)), D((4, CH)), D((4, CH)),
            D((4, CH)), D((4, CH)), D((2, 2)), D((2, 2)), D((groups, NY + NZ - 1)), D((groups, NY + NZ - 1)),
            D((5, NY)), D((5, NY)), D((2,)),
        ]
        wide = jax.ShapeDtypeStruct((T, WD), BF16)
        hbm = pl.BlockSpec(memory_space=pltpu.HBM)
        vmem = pl.BlockSpec(memory_space=pltpu.VMEM)
        ins = (q, k, v, g, clusters, owner_slot)
        outs = pl.pallas_call(
            functools.partial(kernel, dims),
            out_shape=(wide, wide, wide, wide, jax.ShapeDtypeStruct((H, HD), BF16)),
            in_specs=[hbm] * 6,
            out_specs=(vmem,) * 5,
            scratch_shapes=scratch,
            compiler_params=pltpu.CompilerParams(
                collective_id=0, has_side_effects=True, vmem_limit_bytes=40 * 1024 * 1024
            ),
        )(*(pltpu.with_memory_space_constraint(a, pltpu.HBM) for a in ins))
        small = jax.ShapeDtypeStruct((H, HD), BF16)
        outs = pl.pallas_call(
            flush,
            out_shape=(wide, wide, wide, wide, small),
            in_specs=[vmem] * 5,
            out_specs=(hbm,) * 5,
            scratch_shapes=[D((5,))],
            compiler_params=pltpu.CompilerParams(vmem_limit_bytes=8 * 1024 * 1024),
        )(*outs)
        return (*outs[:4], outs[4].reshape(H, 1, HD))

    rows = P(("seq", "head"), None)
    return jax.shard_map(
        body,
        mesh=mesh,
        in_specs=(rows, rows, rows, rows, P("head", "seq"), P("head", None)),
        out_specs=(P("seq", "head"),) * 4 + (P("head", "seq", None),),
        check_vma=False,
    )
```
